128 devices in a mesh: leaf: 8 (over x, core), tile: 16 (over y, z).
Axes of the slice: x: 4, y: 4, z: 4, core: 2. Of those that a mesh axis runs over, the one named last changes fastest.
Arguments:
- forcing_leaf: float32 [8, 4, 16, 64, 128], P('leaf', None, 'tile'), may hold values from -6 to 6
- inverse_leaf: float32 [8, 2, 16, 128, 128], P('leaf', None, 'tile'), may hold values from -0.2 to 2
- dense_leaf: float32 [8, 16, 32, 128, 128], P('leaf', 'tile'), may hold values from -0.25 to 0.25
- slot_leaf: int32 [8, 4, 16, 32], P('leaf', None, 'tile'), may hold values from -1 to 31, as said below
- left_leaf: float32 [8, 4, 16, 32, 32, 128], P('leaf', None, 'tile'), may hold values from -1 to 1
- right_leaf: float32 [8, 4, 16, 32, 32, 128], P('leaf', None, 'tile'), may hold values from -0.25 to 0.25
- rank_leaf: int32 [8, 4, 16, 32], P('leaf', None, 'tile'), may hold values from 1 to 32
- place_leaf: int32 [8, 2, 16], P('leaf', None, 'tile'), may hold values from 0 to 3, as said below
- forcing_root: float32 [4, 16, 64, 128], P(None, 'tile'), may hold values from -6 to 6
- inverse_root: float32 [2, 16, 128, 128], P(None, 'tile'), may hold values from -0.2 to 2
- dense_root: float32 [16, 32, 128, 128], P('tile'), may hold values from -0.25 to 0.25
- slot_root: int32 [4, 16, 32], P(None, 'tile'), may hold values from -1 to 31, as said below
- left_root: float32 [4, 16, 32, 32, 128], P(None, 'tile'), may hold values from -1 to 1
- right_root: float32 [4, 16, 32, 32, 128], P(None, 'tile'), may hold values from -0.25 to 0.25
- rank_root: int32 [4, 16, 32], P(None, 'tile'), may hold values from 1 to 32
Outputs:
- leaf_pivots: float32 [8, 2, 16, 64, 128], P('leaf', None, 'tile')
- root_pivots: float32 [2, 16, 64, 128], P(None, 'tile', 'leaf')
- root_updates: float32 [2, 16, 64, 128], P(None, 'tile', 'leaf')
The draws below stay inside these ranges and needn't reach their ends.
Inputs may be any that keep to these rules, and one draw needn't show every extreme that they name: `slot_leaf`: in the 4 x 32 table of one leaf and one tile index, each of 0 to 31 appears exactly once and all other entries are -1. `slot_root`: in the 4 x 32 table of one tile index, each of 0 to 31 appears exactly once and all other entries are -1. `place_leaf`: the 2 entries of one leaf and one tile index are distinct.
All inputs are finite; a program needn't handle non-finite values.
Results may differ from the reference program's by a relative error of at most 0.0003.
Values sent between devices are 32-bit elements; how exact they have to be, the bound alone decides.
A program may use at most 64 MiB of HBM per device.

```python
import math
import jax
import jax.numpy as jnp
from jax import lax

BLK = 128
RMAX = 32
PIVB = 2
UPDB = 2
SRC = 64
LEAVES = 8
TILES = 16
LOCB = 4
NBP = 32
NDENSE = 32


def inverse_blocks(key, count):
    key_diag, key_off = jax.random.split(key)
    diag_vals = jnp.exp(jax.random.uniform(key_diag, (count, BLK), jnp.float32, math.log(0.5), math.log(2.0)))
    spread = 0.3 / math.sqrt(BLK)
    off_diag = jax.random.normal(key_off, (count, BLK, BLK), jnp.float32) * spread
    off_diag = jnp.clip(off_diag, -0.2, 0.2)
    identity = jnp.eye(BLK, dtype=jnp.float32)
    return off_diag * (1.0 - identity) + identity * diag_vals[:, :, None]


def draw_inverse_leaf(key, part):
    return inverse_blocks(jax.random.fold_in(key, 11), LEAVES * PIVB * TILES).reshape(LEAVES, PIVB, TILES, BLK, BLK)


def draw_inverse_root(key, part):
    return inverse_blocks(jax.random.fold_in(key, 12), PIVB * TILES).reshape(PIVB, TILES, BLK, BLK)


def slot_table(key, count):
    key_list = jax.random.split(key, count)
    shuffled = jax.vmap(lambda one_key: jax.random.permutation(one_key, LOCB * NBP))(key_list)
    positions = jnp.argsort(shuffled, axis=1)
    return jnp.where(positions < NDENSE, positions, -1).astype(jnp.int32).reshape(count, LOCB, NBP)


def draw_slot_leaf(key, part):
    table = slot_table(jax.random.fold_in(key, 21), LEAVES * TILES)
    return table.reshape(LEAVES, TILES, LOCB, NBP).transpose(0, 2, 1, 3)


def draw_slot_root(key, part):
    table = slot_table(jax.random.fold_in(key, 22), TILES)
    return table.transpose(1, 0, 2)


def draw_place_leaf(key, part):
    key_list = jax.random.split(jax.random.fold_in(key, 31), LEAVES * TILES)
    chosen = jax.vmap(lambda one_key: jax.random.permutation(one_key, LOCB)[:UPDB])(key_list)
    return chosen.reshape(LEAVES, TILES, UPDB).transpose(0, 2, 1).astype(jnp.int32)


def with_ends(array, key, smallest, high):
    place = [jax.random.randint(jax.random.fold_in(key, axis), (), 0, length) for axis, length in enumerate(array.shape)]
    widest = array.shape.index(max(array.shape))
    next_to = place[:widest] + [(place[widest] + 1) % array.shape[widest]] + place[widest + 1:]
    return array.at[tuple(place)].set(smallest).at[tuple(next_to)].set(high)


def block_scale(stream_key, shape, cuts, smallest, top_value):
    def one(dim, parts):
        draws = jax.random.uniform(jax.random.fold_in(jax.random.fold_in(stream_key, 6), dim), (parts,), jnp.float32, smallest / len(cuts), top_value / len(cuts))
        return jnp.repeat(jnp.exp(draws), shape[dim] // parts).reshape((-1,) + (1,) * (len(shape) - dim - 1))

    gain = one(*cuts[0])
    for cut in cuts[1:]:
        gain = gain * one(*cut)
    return gain


def bell_draw(stream_key, extent, scale, most, shards=(), held_as=jnp.bfloat16):
    values = scale * jax.random.normal(stream_key, extent, jnp.float32)
    if shards:
        values = values * block_scale(stream_key, extent, shards, -0.22, 0.18)
    return jnp.clip(values, -most, most).astype(held_as)


def setup_inputs(seed: int = 0) -> dict:
    arg_keys = jax.random.split(jax.random.key(seed), 16)
    return {
        "forcing_leaf": bell_draw(arg_keys[0], (LEAVES, LOCB, TILES, SRC, BLK), 1.0, 6.0, ((0, 8), (2, 16)), jnp.float32),
        "inverse_leaf": draw_inverse_leaf(jax.random.fold_in(arg_keys[15], 71), 0),
        "dense_leaf": bell_draw(arg_keys[2], (LEAVES, TILES, NDENSE, BLK, BLK), ((BLK * NBP) ** -0.5), 0.25, ((0, 8), (1, 16)), jnp.float32),
        "slot_leaf": draw_slot_leaf(jax.random.fold_in(arg_keys[15], 71), 0),
        "left_leaf": bell_draw(arg_keys[4], (LEAVES, LOCB, TILES, NBP, RMAX, BLK), RMAX ** -0.5, 1.0, ((0, 8), (2, 16)), jnp.float32),
        "right_leaf": bell_draw(arg_keys[5], (LEAVES, LOCB, TILES, NBP, RMAX, BLK), ((BLK * NBP) ** -0.5), 0.25, ((0, 8), (2, 16)), jnp.float32),
        "rank_leaf": with_ends(jax.random.randint(arg_keys[6], (LEAVES, LOCB, TILES, NBP), 1, RMAX + 1), jax.random.fold_in(arg_keys[6], 1), 1, RMAX).astype(jnp.int32),
        "place_leaf": draw_place_leaf(jax.random.fold_in(arg_keys[15], 71), 0),
        "forcing_root": bell_draw(arg_keys[8], (LOCB, TILES, SRC, BLK), 1.0, 6.0, ((1, 16),), jnp.float32),
        "inverse_root": draw_inverse_root(jax.random.fold_in(arg_keys[15], 71), 0),
        "dense_root": bell_draw(arg_keys[10], (TILES, NDENSE, BLK, BLK), ((BLK * NBP) ** -0.5), 0.25, ((0, 16),), jnp.float32),
        "slot_root": draw_slot_root(jax.random.fold_in(arg_keys[15], 71), 0),
        "left_root": bell_draw(arg_keys[12], (LOCB, TILES, NBP, RMAX, BLK), RMAX ** -0.5, 1.0, ((1, 16),), jnp.float32),
        "right_root": bell_draw(arg_keys[13], (LOCB, TILES, NBP, RMAX, BLK), ((BLK * NBP) ** -0.5), 0.25, ((1, 16),), jnp.float32),
        "rank_root": with_ends(jax.random.randint(arg_keys[14], (LOCB, TILES, NBP), 1, RMAX + 1), jax.random.fold_in(arg_keys[14], 1), 1, RMAX).astype(jnp.int32),
    }


highest = lax.Precision.HIGHEST


def apply_column(tile_set, slot_col, right_col, left_col, rank_col, solved):
    dense_out = jnp.einsum('lij,sj->lsi', tile_set, solved, precision=highest)
    projected = jnp.einsum('lrj,sj->lrs', right_col, solved, precision=highest)
    rank_mask = (jnp.arange(right_col.shape[1], dtype=jnp.int32)[None, :] < rank_col[:, None]).astype(jnp.float32)
    low_out = jnp.einsum('lri,lrs->lsi', left_col, projected * rank_mask[:, :, None], precision=highest)
    return jnp.where((slot_col >= 0)[:, None, None], dense_out, low_out)


def solve_front(forcing, inverse, dense_pool, slot_map, left_fac, right_fac, rank_map):
    group_size = forcing.shape[1]
    blocks = forcing.shape[0] * group_size
    current = forcing.reshape((blocks,) + forcing.shape[2:])
    inv_flat = inverse.reshape((-1,) + inverse.shape[2:])
    slot_flat = slot_map.reshape((blocks, slot_map.shape[2]))
    rank_flat = rank_map.reshape((blocks, rank_map.shape[2]))
    left_flat = left_fac.reshape((blocks,) + left_fac.shape[2:])
    right_flat = right_fac.reshape((blocks,) + right_fac.shape[2:])
    row_ids = jnp.arange(blocks, dtype=jnp.int32)
    owner_tile = row_ids % group_size

    def advance(column, rows_now):
        column = column.astype(jnp.int32)
        pivot_in = lax.dynamic_index_in_dim(rows_now, column, 0, keepdims=False)
        inv_block = lax.dynamic_index_in_dim(inv_flat, column, 0, keepdims=False)
        solved = jnp.einsum('ab,sb->sa', inv_block, pivot_in, precision=highest)
        slot_col = lax.dynamic_index_in_dim(slot_flat, column, 1, keepdims=False)
        rank_col = lax.dynamic_index_in_dim(rank_flat, column, 1, keepdims=False)
        left_col = lax.dynamic_index_in_dim(left_flat, column, 1, keepdims=False)
        right_col = lax.dynamic_index_in_dim(right_flat, column, 1, keepdims=False)
        tile_set = dense_pool[owner_tile, jnp.maximum(slot_col, 0)]
        update = apply_column(tile_set, slot_col, right_col, left_col, rank_col, solved)
        rows_now = jnp.where((row_ids > column)[:, None, None], rows_now - update, rows_now)
        return jnp.where((row_ids == column)[:, None, None], solved[None], rows_now)

    current = lax.fori_loop(0, slot_map.shape[2], advance, current)
    return current.reshape(forcing.shape)


def reference(forcing_leaf, inverse_leaf, dense_leaf, slot_leaf, left_leaf, right_leaf, rank_leaf, place_leaf, forcing_root, inverse_root, dense_root, slot_root, left_root, right_root, rank_root):
    leaf_solved = lax.map(lambda operands: solve_front(*operands), (forcing_leaf, inverse_leaf, dense_leaf, slot_leaf, left_leaf, right_leaf, rank_leaf))
    leaf_pivots = leaf_solved[:, :PIVB]
    updates = leaf_solved[:, PIVB:]
    onehot = (place_leaf[..., None] == jnp.arange(LOCB, dtype=jnp.int32)).astype(jnp.float32)
    gathered_sum = jnp.einsum('gutm,gutsb->mtsb', onehot, updates, precision=highest)
    root_forcing = forcing_root + gathered_sum
    root_solved = solve_front(root_forcing, inverse_root, dense_root, slot_root, left_root, right_root, rank_root)
    return leaf_pivots, root_solved[:PIVB], root_solved[PIVB:]
```

```python
import functools

import jax
import jax.numpy as jnp
from jax import lax
from jax.experimental import pallas as pl
from jax.experimental.pallas import tpu as pltpu
from jax.sharding import PartitionSpec as P

F32 = jnp.float32
BF16 = jnp.bfloat16
MESH = pl.DeviceIdType.MESH


def split(a):
    high = a.astype(BF16)
    return high, (a - high.astype(F32)).astype(BF16)


def dot_nn(a, b):
    return lax.dot_general(a, b, (((1,), (0,)), ((), ())), preferred_element_type=F32)


def dot_nt(a, b):
    return lax.dot_general(a, b, (((1,), (1,)), ((), ())), preferred_element_type=F32)


def mul_nn(a, b):
    ah, al = split(a)
    bh, bl = split(b)
    return dot_nn(jnp.concatenate([ah, al], 1), jnp.concatenate([bh, bh], 0)) + dot_nn(ah, bl)


def mul_nt(x, wh, wl):
    rows = x.shape[0]
    xh = x.astype(BF16)
    xhf = xh.astype(F32)
    both = jnp.concatenate([xhf, x - xhf], 0).astype(BF16)
    first = dot_nt(both, wh)
    return first[:rows] + first[rows:] + dot_nt(xh, wl)


class Front:
    def __init__(self, **refs):
        self.__dict__.update(refs)

    def masked_right(self, l, k):
        right = self.right[l, k]
        row = lax.broadcasted_iota(jnp.int32, right.shape, 0)
        return jnp.where(row < self.rank[0, l, 0, k], right, 0.0)

    def choose(self, l, k, low):
        slot = self.slot[0, l, 0, k]
        dense = self.dense[jnp.maximum(slot, 0)]
        return jnp.where(slot >= 0, dense, low)

    def tile(self, l, k):
        left = self.left[l, k]
        lh = left.astype(BF16).astype(F32)
        rh, rl = split(self.masked_right(l, k))
        zero = jnp.zeros_like(left)
        cols = jnp.concatenate([lh, left - lh, lh, zero], 0).T.astype(BF16)
        rows = jnp.concatenate([rh, rh, rl, zero.astype(BF16)], 0)
        return self.choose(l, k, dot_nn(cols, rows))

    def prepare_column(self, pair, half):
        k = 2 * pair + half
        blocks = self.left.shape[0]
        lt = jnp.concatenate([self.left[l, k] for l in range(blocks)], 0).T
        lh, ll = split(lt)
        rights = [split(self.masked_right(l, k)) for l in range(blocks)]

        def diagonal(part):
            zero = jnp.zeros_like(rights[0][0])
            return jnp.concatenate(
                [
                    jnp.concatenate([rights[l][part] if m == l else zero for m in range(blocks)], 1)
                    for l in range(blocks)
                ],
                0,
            )

        rh, rl = diagonal(0), diagonal(1)
        low = dot_nn(jnp.concatenate([lh, ll], 1), jnp.concatenate([rh, rh], 0)) + dot_nn(lh, rl)
        for l in range(blocks):
            th, tl = split(self.choose(l, k, low[:, 128 * l : 128 * (l + 1)]))
            self.wh[pair, 128 * l : 128 * (l + 1), 128 * half : 128 * (half + 1)] = th
            self.wl[pair, 128 * l : 128 * (l + 1), 128 * half : 128 * (half + 1)] = tl

    def prepare(self, pair):
        self.prepare_column(pair, 0)
        self.prepare_column(pair, 1)

    def send_x(self, l, me, to, order):
        i = l * self.tiles + me
        return pltpu.make_async_remote_copy(
            self.x.at[i], self.x.at[i], self.xs.at[l, order], self.xr.at[i],
            device_id={"tile": to}, device_id_type=MESH,
        )

    def wait_x(self, i):
        pltpu.make_async_remote_copy(
            self.x.at[i], self.x.at[i], self.xs.at[0, 0], self.xr.at[i],
            device_id={"tile": 0}, device_id_type=MESH,
        ).wait_recv()

    def copy_c(self, l, to):
        return pltpu.make_async_remote_copy(
            self.c.at[l], self.cin.at[l], self.cs.at[l], self.cr.at[l],
            device_id={"tile": to}, device_id_type=MESH,
        )

    def copy_p(self, l, to):
        return pltpu.make_async_remote_copy(
            self.pout.at[l], self.pin.at[l], self.ps.at[l], self.pr.at[l],
            device_id={"tile": to}, device_id_type=MESH,
        )

    def previous(self, l, me):
        return jnp.maximum(l * (self.tiles // 2) + me // 2 - 1, 0)

    def start_p(self, l, me):
        prev = self.previous(l, me)
        for half in range(2):
            part = mul_nn(self.inverse[l], self.tile(l, 2 * prev + half))
            cols = slice(128 * half, 128 * (half + 1))
            self.pout[l, :, cols] = part
            self.ph[l, :, cols], self.pl[l, :, cols] = split(part)
        self.copy_p(l, me + 1).start()

    def own_b(self, l, me):
        group = l * (self.tiles // 2) + me // 2
        part = mul_nn(self.inverse[l], self.tile(l, 2 * group))
        self.bmat[l] = part
        self.bh[l], self.bl[l] = split(part)

    def finish_p(self, l, me):
        prev = self.previous(l, me)
        parts = [mul_nn(self.inverse[l], self.tile(l, 2 * prev + half)) for half in range(2)]
        self.copy_p(l, me).wait_recv()
        for half in range(2):
            cols = slice(128 * half, 128 * (half + 1))
            part = parts[half] - mul_nn(self.bmat[l], self.pin[l, :, cols])
            self.ph[l, :, cols], self.pl[l, :, cols] = split(part)

    def start_c(self, l, me):
        dh, dl = split(self.inverse[l])
        self.c[l] = mul_nt(self.b[l], dh, dl)

        @pl.when(me % 2 == 0)
        def _():
            self.copy_c(l, me + 1).start()

    def finish_c(self, l, me):
        self.copy_c(l, me).wait_recv()
        self.c[l] = self.c[l] - mul_nt(self.cin[l], self.bh[l], self.bl[l])

    def emit(self, l, me, solved):
        i = l * self.tiles + me
        self.x[i] = solved
        for order, step in enumerate(self.steps):
            self.send_x(l, me, lax.rem(me + step, self.tiles), order).start()

    def arrive(self, pair, me):
        @pl.when(me // 2 != lax.rem(pair, self.groups))
        def _():
            self.wait_x(2 * pair)
            self.wait_x(2 * pair + 1)

        @pl.when(me // 2 == lax.rem(pair, self.groups))
        def _():
            self.wait_x(2 * pair + 1 - me % 2)

    def pair_now(self, pair):
        return jnp.concatenate([self.x[2 * pair], self.x[2 * pair + 1]], 1)

    def update(self, pair, me):
        out = mul_nt(self.pair_now(pair), self.wh[pair], self.wl[pair])
        for l in range(self.b.shape[0]):
            part = out[:, 128 * l : 128 * (l + 1)]
            if l < 2:
                later = (l * self.groups + me // 2 > pair + 1).astype(F32)
                part = part * later
            self.b[l] = self.b[l] - part

    def wait_sends(self, me):
        for l in range(2):
            for order, step in enumerate(self.steps):
                self.send_x(l, me, lax.rem(me + step, self.tiles), order).wait_send()

        @pl.when(me % 2 == 0)
        def _():
            for l in range(2):
                self.copy_c(l, me + 1).wait_send()
                self.copy_p(l, me + 1).wait_send()


def first_steps(front, me):
    @pl.when(me // 2 < 2)
    def _():
        front.start_c(0, me)

    @pl.when(me == 1)
    def _():
        front.finish_c(0, me)

    @pl.when(me // 2 == 0)
    def _():
        front.emit(0, me, front.c[0])


def run_front(front, me, extra):
    pairs = 2 * front.groups

    def step(pair, carry):
        extra(pair)
        mine_next = jnp.logical_and(pair + 1 < pairs, me // 2 == lax.rem(pair + 1, front.groups))
        mine_then = jnp.logical_and(pair + 2 < pairs, me // 2 == lax.rem(pair + 2, front.groups))
        l_next = lax.rem(pair + 1, pairs) // front.groups
        l_then = lax.rem(pair + 2, pairs) // front.groups

        @pl.when(jnp.logical_and(mine_next, me % 2 == 1))
        def _():
            front.finish_c(l_next, me)

        front.arrive(pair, me)

        @pl.when(mine_next)
        def _():
            solved = mul_nt(front.pair_now(pair), front.ph[l_next], front.pl[l_next])
            front.emit(l_next, me, front.c[l_next] - solved)

        front.update(pair, me)

        @pl.when(mine_then)
        def _():
            front.start_c(l_then, me)

        return carry

    lax.fori_loop(0, pairs, step, 0)


def kernel(sizes, *refs):
    tiles, leaves, blocks, sources = sizes
    share = sources // leaves
    names_in = ("forcing", "inverse", "dense", "slot", "left", "right", "rank")
    leaf_in = dict(zip(names_in, refs[:7]))
    place = refs[7]
    root_in = dict(zip(names_in, refs[8:15]))
    leaf_pivots, root_pivots, root_updates = refs[15:18]
    scratch = list(refs[18:])
    me = lax.axis_index("tile")
    my_leaf = lax.axis_index("leaf")
    order = [2, 1, 3] + [s for s in range(4, tiles)]
    order = [s for s in order if s < tiles]
    if tiles - 1 in order[3:]:
        order.remove(tiles - 1)
        order.insert(4, tiles - 1)

    def front_of(inputs):
        names = (
            "b", "x", "c", "cin", "pout", "pin", "ph", "pl", "bmat", "bh", "bl", "wh", "wl",
            "inverse", "dense", "left", "right",
            "xs", "xr", "cs", "cr", "ps", "pr", "load",
        )
        mine = {name: scratch.pop(0) for name in names}
        return Front(
            slot=inputs["slot"], rank=inputs["rank"], tiles=tiles, groups=tiles // 2,
            steps=order, **mine,
        )

    leaf = front_of(leaf_in)
    root = front_of(root_in)
    root_forcing, sum_out, sum_in, sum_send, sum_recv = scratch

    def load(front, inputs, forcing):
        pairs = [(inputs["forcing"], forcing)] + [
            (inputs[n], getattr(front, n)) for n in ("inverse", "left", "right", "dense")
        ]
        return [
            pltpu.make_async_copy(src, dst, front.load.at[n]) for n, (src, dst) in enumerate(pairs)
        ]

    leaf_loads = load(leaf, leaf_in, leaf.b)
    root_loads = load(root, root_in, root_forcing)
    for copy in leaf_loads:
        copy.start()
    for copy in root_loads:
        copy.start()

    barrier = pltpu.get_barrier_semaphore()
    for step in range(1, tiles):
        pl.semaphore_signal(
            barrier, inc=1, device_id={"tile": lax.rem(me + step, tiles)}, device_id_type=MESH
        )
    for step in range(1, leaves):
        pl.semaphore_signal(
            barrier, inc=1, device_id={"leaf": lax.rem(my_leaf + step, leaves)}, device_id_type=MESH
        )
    for copy in leaf_loads:
        copy.wait()
    pl.semaphore_wait(barrier, tiles + leaves - 2)

    odd = me % 2 == 1
    even = me % 2 == 0

    def setup_first(front):
        @pl.when(even)
        def _():
            front.start_p(0, me)
            front.start_p(1, me)

        @pl.when(odd)
        def _():
            front.own_b(0, me)
            front.own_b(1, me)

    def setup_last(front):
        @pl.when(odd)
        def _():
            front.finish_p(0, me)
            front.finish_p(1, me)

    @pl.when(odd)
    def _():
        leaf.own_b(0, me)

    first_steps(leaf, me)

    @pl.when(even)
    def _():
        leaf.start_p(0, me)
        leaf.start_p(1, me)

    @pl.when(odd)
    def _():
        leaf.own_b(1, me)

    setup_last(leaf)
    for copy in root_loads:
        copy.wait()

    def beside(pair):
        leaf.prepare(pair)
        root.prepare(pair)

        @pl.when(pair == 1)
        def _():
            setup_first(root)

        @pl.when(pair == tiles - 2)
        def _():
            setup_last(root)

    run_front(leaf, me, beside)

    for l in range(2):
        leaf_pivots[l] = leaf.x[l * tiles + me]

    for m in range(blocks):
        part = jnp.zeros((sources, 128), F32)
        for u in range(2):
            part = part + leaf.b[2 + u] * (place[0, u, 0] == m).astype(F32)
        for g in range(leaves):
            sum_out[g, m] = part[share * g : share * (g + 1)]

    def sum_copy(step, there):
        return pltpu.make_async_remote_copy(
            sum_out.at[there], sum_in.at[my_leaf], sum_send.at[step], sum_recv.at[my_leaf],
            device_id={"leaf": there}, device_id_type=MESH,
        )

    def sum_wait(here):
        return pltpu.make_async_remote_copy(
            sum_out.at[here], sum_in.at[here], sum_send.at[0], sum_recv.at[here],
            device_id={"leaf": here}, device_id_type=MESH,
        )

    for step in range(1, leaves):
        sum_copy(step, lax.rem(my_leaf + step, leaves)).start()
    for m in range(blocks):
        mine = root_forcing[m, pl.ds(pl.multiple_of(my_leaf * share, share), share)]
        root.b[m] = mine + sum_out[my_leaf, m]
    for step in range(1, leaves):
        here = lax.rem(my_leaf + step, leaves)
        sum_wait(here).wait_recv()
        for m in range(blocks):
            root.b[m] = root.b[m] + sum_in[here, m]

    first_steps(root, me)
    run_front(root, me, lambda pair: None)
    for l in range(2):
        root_pivots[l] = root.x[l * tiles + me]
        root_updates[l] = root.b[2 + l]

    leaf.wait_sends(me)
    root.wait_sends(me)
    for step in range(1, leaves):
        sum_copy(step, lax.rem(my_leaf + step, leaves)).wait_send()


def front_scratch(tiles, blocks, sources, dense_count, rank):
    pivots = 2 * tiles
    pairs = tiles
    blk = 128
    vmem = pltpu.VMEM
    dma = pltpu.SemaphoreType.DMA
    return [
        vmem((blocks, sources, blk), F32),
        vmem((pivots, sources, blk), F32),
        vmem((2, sources, blk), F32),
        vmem((2, sources, blk), F32),
        vmem((2, blk, 2 * blk), F32),
        vmem((2, blk, 2 * blk), F32),
        vmem((2, blk, 2 * blk), BF16),
        vmem((2, blk, 2 * blk), BF16),
        vmem((2, blk, blk), F32),
        vmem((2, blk, blk), BF16),
        vmem((2, blk, blk), BF16),
        vmem((pairs, blocks * blk, 2 * blk), BF16),
        vmem((pairs, blocks * blk, 2 * blk), BF16),
        vmem((2, blk, blk), F32),
        vmem((dense_count, blk, blk), F32),
        vmem((blocks, pivots, rank, blk), F32),
        vmem((blocks, pivots, rank, blk), F32),
        dma((2, tiles - 1)),
        dma((pivots,)),
        dma((2,)),
        dma((2,)),
        dma((2,)),
        dma((2,)),
        dma((5,)),
    ]


def body(
    forcing_leaf,
    inverse_leaf,
    dense_leaf,
    slot_leaf,
    left_leaf,
    right_leaf,
    rank_leaf,
    place_leaf,
    forcing_root,
    inverse_root,
    dense_root,
    slot_root,
    left_root,
    right_root,
    rank_root,
):
    tiles = lax.axis_size("tile")
    leaves = lax.axis_size("leaf")
    blocks, sources, blk = forcing_leaf.shape[1], forcing_leaf.shape[3], forcing_leaf.shape[4]
    dense_count, rank = dense_leaf.shape[2], left_leaf.shape[4]
    share = sources // leaves
    args = (
        forcing_leaf[0, :, 0],
        inverse_leaf[0, :, 0],
        dense_leaf[0, 0],
        slot_leaf,
        left_leaf[0, :, 0],
        right_leaf[0, :, 0],
        rank_leaf,
        place_leaf,
        forcing_root[:, 0],
        inverse_root[:, 0],
        dense_root[0],
        slot_root[None],
        left_root[:, 0],
        right_root[:, 0],
        rank_root[None],
    )
    smem = pl.BlockSpec(memory_space=pltpu.SMEM)
    hbm = pl.BlockSpec(memory_space=pl.ANY)
    vmem = pl.BlockSpec(memory_space=pltpu.VMEM)
    one = [hbm, hbm, hbm, smem, hbm, hbm, smem]
    leaf_pivots, root_pivots, root_updates = pl.pallas_call(
        functools.partial(kernel, (tiles, leaves, blocks, sources)),
        out_shape=(
            jax.ShapeDtypeStruct((2, sources, blk), F32),
            jax.ShapeDtypeStruct((2, share, blk), F32),
            jax.ShapeDtypeStruct((2, share, blk), F32),
        ),
        in_specs=one + [smem] + one,
        out_specs=(vmem, vmem, vmem),
        scratch_shapes=front_scratch(tiles, blocks, sources, dense_count, rank)
        + front_scratch(tiles, blocks, share, dense_count, rank)
        + [
            pltpu.VMEM((blocks, sources, blk), F32),
            pltpu.VMEM((leaves, blocks, share, blk), F32),
            pltpu.VMEM((leaves, blocks, share, blk), F32),
            pltpu.SemaphoreType.DMA((leaves,)),
            pltpu.SemaphoreType.DMA((leaves,)),
        ],
        compiler_params=pltpu.CompilerParams(
            collective_id=0, has_side_effects=True, vmem_limit_bytes=60 * 2**20
        ),
    )(*args)
    return leaf_pivots[None, :, None], root_pivots[:, None], root_updates[:, None]


def solution(mesh):
    placed = (
        P("leaf", None, "tile", None, None),
        P("leaf", None, "tile", None, None),
        P("leaf", "tile", None, None, None),
        P("leaf", None, "tile", None),
        P("leaf", None, "tile", None, None, None),
        P("leaf", None, "tile", None, None, None),
        P("leaf", None, "tile", None),
        P("leaf", None, "tile"),
        P(None, "tile", None, None),
        P(None, "tile", None, None),
        P("tile", None, None, None),
        P(None, "tile", None),
        P(None, "tile", None, None, None),
        P(None, "tile", None, None, None),
        P(None, "tile", None),
    )
    return jax.shard_map(
        body,
        mesh=mesh,
        in_specs=placed,
        out_specs=(
            P("leaf", None, "tile", None, None),
            P(None, "tile", "leaf", None),
            P(None, "tile", "leaf", None),
        ),
        check_vma=False,
    )
```

```python
import functools

import jax
import jax.numpy as jnp
from jax import lax
from jax.experimental import pallas as pl
from jax.experimental.pallas import tpu as pltpu
from jax.sharding import PartitionSpec as P

F32 = jnp.float32
BF16 = jnp.bfloat16
MESH = pl.DeviceIdType.MESH


def split(a):
    high = a.astype(BF16)
    return high, (a - high.astype(F32)).astype(BF16)


def dot_nn(a, b):
    return lax.dot_general(a, b, (((1,), (0,)), ((), ())), preferred_element_type=F32)


def dot_nt(a, b):
    return lax.dot_general(a, b, (((1,), (1,)), ((), ())), preferred_element_type=F32)


def mul_nn(a, b):
    ah, al = split(a)
    bh, bl = split(b)
    return dot_nn(jnp.concatenate([ah, al], 1), jnp.concatenate([bh, bh], 0)) + dot_nn(ah, bl)


def mul_nt(x, wh, wl):
    rows = x.shape[0]
    xh = x.astype(BF16)
    xhf = xh.astype(F32)
    both = jnp.concatenate([xhf, x - xhf], 0).astype(BF16)
    first = dot_nt(both, wh)
    return first[:rows] + first[rows:] + dot_nt(xh, wl)


class Front:
    def __init__(self, **refs):
        self.__dict__.update(refs)

    def masked_right(self, l, k):
        right = self.right[l, k]
        row = lax.broadcasted_iota(jnp.int32, right.shape, 0)
        return jnp.where(row < self.rank[0, l, 0, k], right, 0.0)

    def choose(self, l, k, low):
        slot = self.slot[0, l, 0, k]
        dense = self.dense[jnp.maximum(slot, 0)]
        return jnp.where(slot >= 0, dense, low)

    def tile(self, l, k):
        left = self.left[l, k]
        lh = left.astype(BF16).astype(F32)
        rh, rl = split(self.masked_right(l, k))
        zero = jnp.zeros_like(left)
        cols = jnp.concatenate([lh, left - lh, lh, zero], 0).T.astype(BF16)
        rows = jnp.concatenate([rh, rh, rl, zero.astype(BF16)], 0)
        return self.choose(l, k, dot_nn(cols, rows))

    def prepare_column(self, pair, half):
        k = 2 * pair + half
        blocks = self.left.shape[0]
        lt = jnp.concatenate([self.left[l, k] for l in range(blocks)], 0).T
        lh, ll = split(lt)
        rights = [split(self.masked_right(l, k)) for l in range(blocks)]

        def diagonal(part):
            zero = jnp.zeros_like(rights[0][0])
            return jnp.concatenate(
                [
                    jnp.concatenate([rights[l][part] if m == l else zero for m in range(blocks)], 1)
                    for l in range(blocks)
                ],
                0,
            )

        rh, rl = diagonal(0), diagonal(1)
        low = dot_nn(jnp.concatenate([lh, ll], 1), jnp.concatenate([rh, rh], 0)) + dot_nn(lh, rl)
        for l in range(blocks):
            th, tl = split(self.choose(l, k, low[:, 128 * l : 128 * (l + 1)]))
            self.wh[pair, 128 * l : 128 * (l + 1), 128 * half : 128 * (half + 1)] = th
            self.wl[pair, 128 * l : 128 * (l + 1), 128 * half : 128 * (half + 1)] = tl

    def prepare(self, pair):
        self.prepare_column(pair, 0)
        self.prepare_column(pair, 1)

    def send_x(self, l, me, to, order):
        i = l * self.tiles + me
        return pltpu.make_async_remote_copy(
            self.x.at[i], self.x.at[i], self.xs.at[l, order], self.xr.at[i],
            device_id={"tile": to}, device_id_type=MESH,
        )

    def wait_x(self, i):
        pltpu.make_async_remote_copy(
            self.x.at[i], self.x.at[i], self.xs.at[0, 0], self.xr.at[i],
            device_id={"tile": 0}, device_id_type=MESH,
        ).wait_recv()

    def copy_c(self, l, to):
        return pltpu.make_async_remote_copy(
            self.c.at[l], self.cin.at[l], self.cs.at[l], self.cr.at[l],
            device_id={"tile": to}, device_id_type=MESH,
        )

    def copy_p(self, l, to):
        return pltpu.make_async_remote_copy(
            self.pout.at[l], self.pin.at[l], self.ps.at[l], self.pr.at[l],
            device_id={"tile": to}, device_id_type=MESH,
        )

    def previous(self, l, me):
        return jnp.maximum(l * (self.tiles // 2) + me // 2 - 1, 0)

    def start_p(self, l, me):
        prev = self.previous(l, me)
        for half in range(2):
            part = mul_nn(self.inverse[l], self.tile(l, 2 * prev + half))
            cols = slice(128 * half, 128 * (half + 1))
            self.pout[l, :, cols] = part
            self.ph[l, :, cols], self.pl[l, :, cols] = split(part)
        self.copy_p(l, me + 1).start()

    def own_b(self, l, me):
        group = l * (self.tiles // 2) + me // 2
        part = mul_nn(self.inverse[l], self.tile(l, 2 * group))
        self.bmat[l] = part
        self.bh[l], self.bl[l] = split(part)

    def finish_p(self, l, me):
        prev = self.previous(l, me)
        parts = [mul_nn(self.inverse[l], self.tile(l, 2 * prev + half)) for half in range(2)]
        self.copy_p(l, me).wait_recv()
        for half in range(2):
            cols = slice(128 * half, 128 * (half + 1))
            part = parts[half] - mul_nn(self.bmat[l], self.pin[l, :, cols])
            self.ph[l, :, cols], self.pl[l, :, cols] = split(part)

    def start_c(self, l, me):
        dh, dl = split(self.inverse[l])
        self.c[l] = mul_nt(self.b[l], dh, dl)

        @pl.when(me % 2 == 0)
        def _():
            self.copy_c(l, me + 1).start()

    def finish_c(self, l, me):
        self.copy_c(l, me).wait_recv()
        self.c[l] = self.c[l] - mul_nt(self.cin[l], self.bh[l], self.bl[l])

    def emit(self, l, me, solved):
        i = l * self.tiles + me
        self.x[i] = solved
        for order, step in enumerate(self.steps):
            self.send_x(l, me, lax.rem(me + step, self.tiles), order).start()

    def arrive(self, pair, me):
        @pl.when(me // 2 != lax.rem(pair, self.groups))
        def _():
            self.wait_x(2 * pair)
            self.wait_x(2 * pair + 1)

        @pl.when(me // 2 == lax.rem(pair, self.groups))
        def _():
            self.wait_x(2 * pair + 1 - me % 2)

    def pair_now(self, pair):
        return jnp.concatenate([self.x[2 * pair], self.x[2 * pair + 1]], 1)

    def update(self, pair, me):
        out = mul_nt(self.pair_now(pair), self.wh[pair], self.wl[pair])
        for l in range(self.b.shape[0]):
            part = out[:, 128 * l : 128 * (l + 1)]
            if l < 2:
                later = (l * self.groups + me // 2 > pair + 1).astype(F32)
                part = part * later
            self.b[l] = self.b[l] - part

    def wait_sends(self, me):
        for l in range(2):
            for order, step in enumerate(self.steps):
                self.send_x(l, me, lax.rem(me + step, self.tiles), order).wait_send()

        @pl.when(me % 2 == 0)
        def _():
            for l in range(2):
                self.copy_c(l, me + 1).wait_send()
                self.copy_p(l, me + 1).wait_send()


SPAN = 4


class Root(Front):
    def place(self, me):
        return me // SPAN, lax.rem(me, SPAN)

    def z_tile(self, l, q, to, back):
        return pltpu.make_async_remote_copy(
            self.zall.at[l, self.my_leaf], self.zin.at[l, q], self.zs.at[l, back], self.zr.at[l, q],
            device_id={"tile": to}, device_id_type=MESH,
        )

    def z_leaf(self, l, step):
        there = lax.rem(self.my_leaf + step, self.leaves)
        return pltpu.make_async_remote_copy(
            self.zall.at[l, self.my_leaf], self.zall.at[l, self.my_leaf],
            self.gs.at[l, step], self.gr.at[l, self.my_leaf],
            device_id={"leaf": there}, device_id_type=MESH,
        )

    def solve_z(self, l, me):
        y, q = self.place(me)
        group = l * self.groups + y
        column = SPAN * jnp.maximum(group - 1, 0) + jnp.minimum(self.my_leaf, SPAN - 1)
        shape = (128, 128)
        same = lax.broadcasted_iota(jnp.int32, shape, 0) == lax.broadcasted_iota(jnp.int32, shape, 1)
        unit = same.astype(F32) * (self.my_leaf - SPAN == q).astype(F32)
        self.zwork[...] = jnp.where(self.my_leaf < SPAN, self.tile(l, column), unit)
        for before in range(SPAN - 1):
            @pl.when(before < q)
            def _(before=before):
                inner = self.tile(l, SPAN * group + before)
                self.z_tile(l, before, me, 0).wait_recv()
                self.zwork[...] = self.zwork[...] - mul_nn(inner, self.zin[l, before])

        self.zall[l, self.my_leaf] = mul_nn(self.inverse[l], self.zwork[...])
        for step in range(1, SPAN):
            @pl.when(q + step < SPAN)
            def _(step=step):
                self.z_tile(l, q, me + step, step).start()

        for step in range(1, self.leaves):
            self.z_leaf(l, step).start()

    def take_z(self, l):
        for g in range(2 * SPAN):
            @pl.when(self.my_leaf != g)
            def _(g=g):
                pltpu.make_async_remote_copy(
                    self.zall.at[l, g], self.zall.at[l, g], self.gs.at[l, 0], self.gr.at[l, g],
                    device_id={"leaf": 0}, device_id_type=MESH,
                ).wait_recv()

            at = slice(128 * (g % SPAN), 128 * (g % SPAN + 1))
            if g < SPAN:
                self.ph[l, :, at], self.pl[l, :, at] = split(self.zall[l, g])
            else:
                self.gh[l, :, at], self.gl[l, :, at] = split(self.zall[l, g])

    def clear(self, me):
        q = lax.rem(me, SPAN)
        for l in range(2):
            for other in range(SPAN):
                @pl.when(other > q)
                def _(l=l, other=other):
                    self.bin[l, other] = jnp.zeros_like(self.bin[l, other])

    def routes(self, me):
        y, q = self.place(me)
        for down in [1, 0] + list(range(2, self.groups)):
            for right in (2, 1, 3, 0):
                if down % self.groups or right:
                    to = lax.rem(y + down, self.groups) * SPAN + lax.rem(q + right, SPAN)
                    yield (down % self.groups) * SPAN + right, to

    def emit(self, l, me, solved):
        self.x[l * self.tiles + me] = solved
        for order, to in self.routes(me):
            self.send_x(l, me, to, order).start()

    def copy_b(self, l, q, to, step):
        return pltpu.make_async_remote_copy(
            self.bin.at[l, q], self.bin.at[l, q], self.bs.at[l, step], self.br.at[l, q],
            device_id={"tile": to}, device_id_type=MESH,
        )

    def start_c(self, l, me):
        q = lax.rem(me, SPAN)
        self.bin[l, q] = self.b[l]
        for step in range(1, SPAN):
            @pl.when(q + step < SPAN)
            def _(step=step):
                self.copy_b(l, q, me + step, step).start()

    def finish_c(self, l, me):
        q = lax.rem(me, SPAN)
        for before in range(SPAN - 1):
            @pl.when(before < q)
            def _(before=before):
                self.copy_b(l, before, me, 0).wait_recv()

        whole = jnp.concatenate([self.bin[l, other] for other in range(SPAN)], 1)
        self.c[l] = mul_nt(whole, self.gh[l], self.gl[l])

    def arrive(self, group, me):
        for n in range(SPAN):
            i = SPAN * group + n
            @pl.when(me != lax.rem(i, self.tiles))
            def _(i=i):
                self.wait_x(i)

    def group_now(self, group):
        return jnp.concatenate([self.x[SPAN * group + n] for n in range(SPAN)], 1)

    def update(self, group, me):
        now = self.group_now(group)
        out = mul_nt(now[:, :256], self.wh[2 * group], self.wl[2 * group])
        out = out + mul_nt(now[:, 256:], self.wh[2 * group + 1], self.wl[2 * group + 1])
        for l in range(self.b.shape[0]):
            part = out[:, 128 * l : 128 * (l + 1)]
            if l < 2:
                part = part * (l * self.groups + me // SPAN > group + 1).astype(F32)
            self.b[l] = self.b[l] - part

    def run(self, me):
        groups = 2 * self.groups
        y = me // SPAN

        @pl.when(y < 2)
        def _():
            self.start_c(0, me)

        @pl.when(y == 0)
        def _():
            self.finish_c(0, me)
            self.emit(0, me, self.c[0])

        def step(group, carry):
            mine_next = jnp.logical_and(group + 1 < groups, y == lax.rem(group + 1, self.groups))
            mine_then = jnp.logical_and(group + 2 < groups, y == lax.rem(group + 2, self.groups))
            l_next = lax.rem(group + 1, groups) // self.groups
            l_then = lax.rem(group + 2, groups) // self.groups

            @pl.when(mine_next)
            def _():
                self.finish_c(l_next, me)

            self.arrive(group, me)

            @pl.when(mine_next)
            def _():
                solved = mul_nt(self.group_now(group), self.ph[l_next], self.pl[l_next])
                self.emit(l_next, me, self.c[l_next] - solved)

            self.update(group, me)

            @pl.when(mine_then)
            def _():
                self.start_c(l_then, me)

            return carry

        lax.fori_loop(0, groups, step, 0)

    def wait_sends(self, me):
        y, q = self.place(me)
        for l in range(2):
            for order, to in self.routes(me):
                self.send_x(l, me, to, order).wait_send()
            for step in range(1, SPAN):
                @pl.when(q + step < SPAN)
                def _(l=l, step=step):
                    self.copy_b(l, q, me + step, step).wait_send()
                    self.z_tile(l, q, me + step, step).wait_send()

            for step in range(1, self.leaves):
                self.z_leaf(l, step).wait_send()


def first_steps(front, me):
    @pl.when(me // 2 < 2)
    def _():
        front.start_c(0, me)

    @pl.when(me == 1)
    def _():
        front.finish_c(0, me)

    @pl.when(me // 2 == 0)
    def _():
        front.emit(0, me, front.c[0])


def run_front(front, me, extra):
    pairs = 2 * front.groups

    def step(pair, carry):
        extra(pair)
        mine_next = jnp.logical_and(pair + 1 < pairs, me // 2 == lax.rem(pair + 1, front.groups))
        mine_then = jnp.logical_and(pair + 2 < pairs, me // 2 == lax.rem(pair + 2, front.groups))
        l_next = lax.rem(pair + 1, pairs) // front.groups
        l_then = lax.rem(pair + 2, pairs) // front.groups

        @pl.when(jnp.logical_and(mine_next, me % 2 == 1))
        def _():
            front.finish_c(l_next, me)

        front.arrive(pair, me)

        @pl.when(mine_next)
        def _():
            solved = mul_nt(front.pair_now(pair), front.ph[l_next], front.pl[l_next])
            front.emit(l_next, me, front.c[l_next] - solved)

        front.update(pair, me)

        @pl.when(mine_then)
        def _():
            front.start_c(l_then, me)

        return carry

    lax.fori_loop(0, pairs, step, 0)


def kernel(sizes, *refs):
    tiles, leaves, blocks, sources = sizes
    share = sources // leaves
    names_in = ("forcing", "inverse", "dense", "slot", "left", "right", "rank")
    leaf_in = dict(zip(names_in, refs[:7]))
    place = refs[7]
    root_in = dict(zip(names_in, refs[8:15]))
    leaf_pivots, root_pivots, root_updates = refs[15:18]
    scratch = list(refs[18:])
    me = lax.axis_index("tile")
    my_leaf = lax.axis_index("leaf")
    order = [2, 1, 3] + [s for s in range(4, tiles)]
    order = [s for s in order if s < tiles]
    if tiles - 1 in order[3:]:
        order.remove(tiles - 1)
        order.insert(4, tiles - 1)

    common = (
        "b", "x", "c", "wh", "wl", "inverse", "dense", "left", "right", "xs", "xr", "load", "ph", "pl",
    )
    for_leaf = ("cin", "pout", "pin", "bmat", "bh", "bl", "cs", "cr", "ps", "pr")
    for_root = (
        "gh", "gl", "bin", "zin", "zall", "zwork", "zs", "zr", "gs", "gr", "bs", "br",
    )

    def front_of(kind, inputs, names, groups, **more):
        mine = {name: scratch.pop(0) for name in names}
        return kind(
            slot=inputs["slot"], rank=inputs["rank"], tiles=tiles, groups=groups, **more, **mine
        )

    leaf = front_of(Front, leaf_in, common + for_leaf, tiles // 2, steps=order)
    root = front_of(
        Root, root_in, common + for_root, tiles // SPAN, leaves=leaves, my_leaf=my_leaf
    )
    root_forcing, sum_out, sum_in, sum_send, sum_recv = scratch

    def load(front, inputs, forcing):
        pairs = [(inputs["forcing"], forcing)] + [
            (inputs[n], getattr(front, n)) for n in ("inverse", "left", "right", "dense")
        ]
        return [
            pltpu.make_async_copy(src, dst, front.load.at[n]) for n, (src, dst) in enumerate(pairs)
        ]

    leaf_loads = load(leaf, leaf_in, leaf.b)
    root_loads = load(root, root_in, root_forcing)
    for copy in leaf_loads:
        copy.start()
    for copy in root_loads:
        copy.start()

    barrier = pltpu.get_barrier_semaphore()
    for step in range(1, tiles):
        pl.semaphore_signal(
            barrier, inc=1, device_id={"tile": lax.rem(me + step, tiles)}, device_id_type=MESH
        )
    for step in range(1, leaves):
        pl.semaphore_signal(
            barrier, inc=1, device_id={"leaf": lax.rem(my_leaf + step, leaves)}, device_id_type=MESH
        )
    for copy in leaf_loads:
        copy.wait()
    pl.semaphore_wait(barrier, tiles + leaves - 2)

    odd = me % 2 == 1
    even = me % 2 == 0

    @pl.when(odd)
    def _():
        leaf.own_b(0, me)

    first_steps(leaf, me)

    @pl.when(even)
    def _():
        leaf.start_p(0, me)
        leaf.start_p(1, me)

    @pl.when(odd)
    def _():
        leaf.own_b(1, me)

    @pl.when(odd)
    def _():
        leaf.finish_p(0, me)
        leaf.finish_p(1, me)

    root.clear(me)
    for copy in root_loads:
        copy.wait()

    def beside(pair):
        leaf.prepare(pair)
        root.prepare(pair)

        @pl.when(pair == 1 + 2 * lax.rem(me, SPAN))
        def _():
            root.solve_z(0, me)
            root.solve_z(1, me)

        @pl.when(pair == tiles - 3)
        def _():
            root.take_z(0)
            root.take_z(1)

    run_front(leaf, me, beside)

    for l in range(2):
        leaf_pivots[l] = leaf.x[l * tiles + me]

    for m in range(blocks):
        part = jnp.zeros((sources, 128), F32)
        for u in range(2):
            part = part + leaf.b[2 + u] * (place[0, u, 0] == m).astype(F32)
        for g in range(leaves):
            sum_out[g, m] = part[share * g : share * (g + 1)]

    def sum_copy(step, there):
        return pltpu.make_async_remote_copy(
            sum_out.at[there], sum_in.at[my_leaf], sum_send.at[step], sum_recv.at[my_leaf],
            device_id={"leaf": there}, device_id_type=MESH,
        )

    def sum_wait(here):
        return pltpu.make_async_remote_copy(
            sum_out.at[here], sum_in.at[here], sum_send.at[0], sum_recv.at[here],
            device_id={"leaf": here}, device_id_type=MESH,
        )

    for step in range(1, leaves):
        sum_copy(step, lax.rem(my_leaf + step, leaves)).start()
    for m in range(blocks):
        mine = root_forcing[m, pl.ds(pl.multiple_of(my_leaf * share, share), share)]
        root.b[m] = mine + sum_out[my_leaf, m]
    for step in range(1, leaves):
        here = lax.rem(my_leaf + step, leaves)
        sum_wait(here).wait_recv()
        for m in range(blocks):
            root.b[m] = root.b[m] + sum_in[here, m]

    root.run(me)
    for l in range(2):
        root_pivots[l] = root.x[l * tiles + me]
        root_updates[l] = root.b[2 + l]

    leaf.wait_sends(me)
    root.wait_sends(me)
    for step in range(1, leaves):
        sum_copy(step, lax.rem(my_leaf + step, leaves)).wait_send()


def common_scratch(tiles, blocks, sources, dense_count, rank, span):
    pivots = 2 * tiles
    blk = 128
    vmem = pltpu.VMEM
    dma = pltpu.SemaphoreType.DMA
    return [
        vmem((blocks, sources, blk), F32),
        vmem((pivots, sources, blk), F32),
        vmem((2, sources, blk), F32),
        vmem((tiles, blocks * blk, 2 * blk), BF16),
        vmem((tiles, blocks * blk, 2 * blk), BF16),
        vmem((2, blk, blk), F32),
        vmem((dense_count, blk, blk), F32),
        vmem((blocks, pivots, rank, blk), F32),
        vmem((blocks, pivots, rank, blk), F32),
        dma((2, tiles)),
        dma((pivots,)),
        dma((5,)),
        vmem((2, blk, span * blk), BF16),
        vmem((2, blk, span * blk), BF16),
    ]


def leaf_scratch(sources):
    blk = 128
    vmem = pltpu.VMEM
    dma = pltpu.SemaphoreType.DMA
    return [
        vmem((2, sources, blk), F32),
        vmem((2, blk, 2 * blk), F32),
        vmem((2, blk, 2 * blk), F32),
        vmem((2, blk, blk), F32),
        vmem((2, blk, blk), BF16),
        vmem((2, blk, blk), BF16),
        dma((2,)),
        dma((2,)),
        dma((2,)),
        dma((2,)),
    ]


def root_scratch(sources, leaves):
    blk = 128
    vmem = pltpu.VMEM
    dma = pltpu.SemaphoreType.DMA
    return [
        vmem((2, blk, SPAN * blk), BF16),
        vmem((2, blk, SPAN * blk), BF16),
        vmem((2, SPAN, sources, blk), F32),
        vmem((2, SPAN, blk, blk), F32),
        vmem((2, leaves, blk, blk), F32),
        vmem((blk, blk), F32),
        dma((2, SPAN)),
        dma((2, SPAN)),
        dma((2, leaves)),
        dma((2, leaves)),
        dma((2, SPAN)),
        dma((2, SPAN)),
    ]


def body(
    forcing_leaf,
    inverse_leaf,
    dense_leaf,
    slot_leaf,
    left_leaf,
    right_leaf,
    rank_leaf,
    place_leaf,
    forcing_root,
    inverse_root,
    dense_root,
    slot_root,
    left_root,
    right_root,
    rank_root,
):
    tiles = lax.axis_size("tile")
    leaves = lax.axis_size("leaf")
    blocks, sources, blk = forcing_leaf.shape[1], forcing_leaf.shape[3], forcing_leaf.shape[4]
    dense_count, rank = dense_leaf.shape[2], left_leaf.shape[4]
    share = sources // leaves
    args = (
        forcing_leaf[0, :, 0],
        inverse_leaf[0, :, 0],
        dense_leaf[0, 0],
        slot_leaf,
        left_leaf[0, :, 0],
        right_leaf[0, :, 0],
        rank_leaf,
        place_leaf,
        forcing_root[:, 0],
        inverse_root[:, 0],
        dense_root[0],
        slot_root[None],
        left_root[:, 0],
        right_root[:, 0],
        rank_root[None],
    )
    smem = pl.BlockSpec(memory_space=pltpu.SMEM)
    hbm = pl.BlockSpec(memory_space=pl.ANY)
    vmem = pl.BlockSpec(memory_space=pltpu.VMEM)
    one = [hbm, hbm, hbm, smem, hbm, hbm, smem]
    leaf_pivots, root_pivots, root_updates = pl.pallas_call(
        functools.partial(kernel, (tiles, leaves, blocks, sources)),
        out_shape=(
            jax.ShapeDtypeStruct((2, sources, blk), F32),
            jax.ShapeDtypeStruct((2, share, blk), F32),
            jax.ShapeDtypeStruct((2, share, blk), F32),
        ),
        in_specs=one + [smem] + one,
        out_specs=(vmem, vmem, vmem),
        scratch_shapes=common_scratch(tiles, blocks, sources, dense_count, rank, 2)
        + leaf_scratch(sources)
        + common_scratch(tiles, blocks, share, dense_count, rank, SPAN)
        + root_scratch(share, leaves)
        + [
            pltpu.VMEM((blocks, sources, blk), F32),
            pltpu.VMEM((leaves, blocks, share, blk), F32),
            pltpu.VMEM((leaves, blocks, share, blk), F32),
            pltpu.SemaphoreType.DMA((leaves,)),
            pltpu.SemaphoreType.DMA((leaves,)),
        ],
        compiler_params=pltpu.CompilerParams(
            collective_id=0, has_side_effects=True, vmem_limit_bytes=60 * 2**20
        ),
    )(*args)
    return leaf_pivots[None, :, None], root_pivots[:, None], root_updates[:, None]


def solution(mesh):
    placed = (
        P("leaf", None, "tile", None, None),
        P("leaf", None, "tile", None, None),
        P("leaf", "tile", None, None, None),
        P("leaf", None, "tile", None),
        P("leaf", None, "tile", None, None, None),
        P("leaf", None, "tile", None, None, None),
        P("leaf", None, "tile", None),
        P("leaf", None, "tile"),
        P(None, "tile", None, None),
        P(None, "tile", None, None),
        P("tile", None, None, None),
        P(None, "tile", None),
        P(None, "tile", None, None, None),
        P(None, "tile", None, None, None),
        P(None, "tile", None),
    )
    return jax.shard_map(
        body,
        mesh=mesh,
        in_specs=placed,
        out_specs=(
            P("leaf", None, "tile", None, None),
            P(None, "tile", "leaf", None),
            P(None, "tile", "leaf", None),
        ),
        check_vma=False,
    )
```

```python
import functools

import jax
import jax.numpy as jnp
from jax import lax
from jax.experimental import pallas as pl
from jax.experimental.pallas import tpu as pltpu
from jax.sharding import PartitionSpec as P

F32 = jnp.float32
BF16 = jnp.bfloat16
MESH = pl.DeviceIdType.MESH


def split(a):
    high = a.astype(BF16)
    return high, (a - high.astype(F32)).astype(BF16)


def dot_nn(a, b):
    return lax.dot_general(a, b, (((1,), (0,)), ((), ())), preferred_element_type=F32)


def dot_nt(a, b):
    return lax.dot_general(a, b, (((1,), (1,)), ((), ())), preferred_element_type=F32)


def mul_nn(a, b):
    ah, al = split(a)
    bh, bl = split(b)
    return dot_nn(jnp.concatenate([ah, al], 1), jnp.concatenate([bh, bh], 0)) + dot_nn(ah, bl)


def mul_nt(x, wh, wl):
    rows = x.shape[0]
    xh = x.astype(BF16)
    xhf = xh.astype(F32)
    both = jnp.concatenate([xhf, x - xhf], 0).astype(BF16)
    first = dot_nt(both, wh)
    return first[:rows] + first[rows:] + dot_nt(xh, wl)


class Front:
    def __init__(self, **refs):
        self.__dict__.update(refs)

    def masked_right(self, l, k):
        right = self.right[l, k]
        row = lax.broadcasted_iota(jnp.int32, right.shape, 0)
        return jnp.where(row < self.rank[0, l, 0, k], right, 0.0)

    def choose(self, l, k, low):
        slot = self.slot[0, l, 0, k]
        dense = self.dense[jnp.maximum(slot, 0)]
        return jnp.where(slot >= 0, dense, low)

    def tile(self, l, k):
        left = self.left[l, k]
        lh = left.astype(BF16).astype(F32)
        rh, rl = split(self.masked_right(l, k))
        zero = jnp.zeros_like(left)
        cols = jnp.concatenate([lh, left - lh, lh, zero], 0).T.astype(BF16)
        rows = jnp.concatenate([rh, rh, rl, zero.astype(BF16)], 0)
        return self.choose(l, k, dot_nn(cols, rows))

    def prepare_column(self, pair, half):
        k = 2 * pair + half
        blocks = self.left.shape[0]
        lt = jnp.concatenate([self.left[l, k] for l in range(blocks)], 0).T
        lh, ll = split(lt)
        rights = [split(self.masked_right(l, k)) for l in range(blocks)]

        def diagonal(part):
            zero = jnp.zeros_like(rights[0][0])
            return jnp.concatenate(
                [
                    jnp.concatenate([rights[l][part] if m == l else zero for m in range(blocks)], 1)
                    for l in range(blocks)
                ],
                0,
            )

        rh, rl = diagonal(0), diagonal(1)
        low = dot_nn(jnp.concatenate([lh, ll], 1), jnp.concatenate([rh, rh], 0)) + dot_nn(lh, rl)
        for l in range(blocks):
            th, tl = split(self.choose(l, k, low[:, 128 * l : 128 * (l + 1)]))
            self.wh[pair, 128 * l : 128 * (l + 1), 128 * half : 128 * (half + 1)] = th
            self.wl[pair, 128 * l : 128 * (l + 1), 128 * half : 128 * (half + 1)] = tl

    def prepare(self, pair):
        self.prepare_column(pair, 0)
        self.prepare_column(pair, 1)


class Leaf(Front):
    def partner(self, me):
        return me + 1 - 2 * lax.rem(me, 2)

    def side(self, me):
        return lax.rem(lax.rem(me, 4) + 1, 4) // 2

    def rows(self, side):
        return pl.ds(pl.multiple_of(side * self.half, self.half), self.half)

    def targets(self, me):
        odd = lax.rem(me, 2)
        for order, (to_even, to_odd) in enumerate(self.steps):
            yield order, lax.rem(me + to_even + (to_odd - to_even) * odd, self.tiles)

    def piece(self, pair, side, to, sem):
        part = self.x.at[pair, self.rows(side)]
        return pltpu.make_async_remote_copy(
            part, part, sem, self.xr.at[2 * pair + side],
            device_id={"tile": to}, device_id_type=MESH,
        )

    def send(self, source, target, sends, recvs, at, me):
        return pltpu.make_async_remote_copy(
            source, target, sends.at[at], recvs.at[at],
            device_id={"tile": self.partner(me)}, device_id_type=MESH,
        )

    def copy_d(self, l, me):
        return self.send(self.inverse.at[l], self.dother.at[l], self.ds, self.dr, l, me)

    def copy_t(self, l, me):
        return self.send(self.inner.at[l], self.inner.at[l], self.ts, self.tr, l, me)

    def copy_r(self, l, q, me):
        return pltpu.make_async_remote_copy(
            self.outer.at[l, q], self.outer.at[l, q], self.rs.at[l], self.rr.at[l],
            device_id={"tile": self.partner(me)}, device_id_type=MESH,
        )

    def copy_b(self, l, q, me):
        return pltpu.make_async_remote_copy(
            self.bout.at[l], self.bin.at[l, q], self.bs.at[l], self.br.at[l],
            device_id={"tile": self.partner(me)}, device_id_type=MESH,
        )

    def share_inner(self, l, me):
        self.copy_d(l, me).start()

        @pl.when(lax.rem(me, 2) == 1)
        def _():
            self.inner[l] = self.tile(l, 2 * (l * self.groups + me // 2))
            self.copy_t(l, me).start()

    def share_outer(self, l, me):
        prev = jnp.maximum(l * self.groups + me // 2 - 1, 0)
        q = lax.rem(me, 2)
        for half in range(2):
            self.outer[l, q, :, 128 * half : 128 * (half + 1)] = self.tile(l, 2 * prev + half)
        self.copy_r(l, q, me).start()

    def diagonals(self, l, me):
        even = lax.rem(me, 2) == 0
        mine, other = self.inverse[l], self.dother[l]
        return jnp.where(even, mine, other), jnp.where(even, other, mine)

    def make_g(self, l, me):
        self.copy_d(l, me).wait_recv()

        @pl.when(lax.rem(me, 2) == 0)
        def _():
            self.copy_t(l, me).wait_recv()

        first, second = self.diagonals(l, me)
        between = mul_nn(second, self.inner[l])
        self.bmat[l] = between
        zero = jnp.zeros((128, 128), BF16)
        low = split(-mul_nn(between, first))
        for ref, top, left, right in zip((self.gh, self.gl), split(first), low, split(second)):
            ref[l, :128, :128] = top
            ref[l, :128, 128:] = zero
            ref[l, 128:, :128] = left
            ref[l, 128:, 128:] = right

    def make_p(self, l, me):
        self.copy_r(l, 1 - lax.rem(me, 2), me).wait_recv()
        first, second = self.diagonals(l, me)
        top = mul_nn(first, self.outer[l, 0])
        bottom = mul_nn(second, self.outer[l, 1]) - mul_nn(self.bmat[l], top)
        self.ph[l, :128], self.pl[l, :128] = split(top)
        self.ph[l, 128:], self.pl[l, 128:] = split(bottom)

    def start_c(self, l, me):
        q, side = lax.rem(me, 2), self.side(me)
        self.bout[l] = self.b[l, self.rows(1 - side)]
        self.copy_b(l, q, me).start()
        self.bin[l, q] = self.b[l, self.rows(side)]

    def finish_c(self, l, me):
        self.copy_b(l, lax.rem(me, 2), me).wait_recv()
        whole = jnp.concatenate([self.bin[l, 0], self.bin[l, 1]], 1)
        self.c[l] = mul_nt(whole, self.gh[l], self.gl[l])

    def emit(self, l, me, solved):
        pair, side = l * self.groups + me // 2, self.side(me)
        self.x[pair, self.rows(side)] = solved
        for order, to in self.targets(me):
            self.piece(pair, side, to, self.xs.at[l, order]).start()

    def wait_piece(self, pair, side):
        self.piece(pair, side, 0, self.xs.at[0, 0]).wait_recv()

    def update(self, pair, me):
        out = mul_nt(self.x[pair], self.wh[pair], self.wl[pair])
        for l in range(self.b.shape[0]):
            part = out[:, 128 * l : 128 * (l + 1)]
            if l < 2:
                part = part * (l * self.groups + me // 2 > pair + 1).astype(F32)
            self.b[l] = self.b[l] - part

    def start(self, me):
        mine = me // 2
        self.share_inner(0, me)

        @pl.when(mine < 2)
        def _():
            self.start_c(0, me)

        self.share_outer(0, me)
        self.make_g(0, me)

        @pl.when(mine == 0)
        def _():
            self.finish_c(0, me)
            self.emit(0, me, self.c[0])

        self.make_p(0, me)

    def run(self, me, extra):
        pairs = 2 * self.groups
        mine, side = me // 2, self.side(me)

        def step(pair, carry):
            extra(pair)
            mine_next = jnp.logical_and(pair + 1 < pairs, mine == lax.rem(pair + 1, self.groups))
            mine_then = jnp.logical_and(pair + 2 < pairs, mine == lax.rem(pair + 2, self.groups))
            l_next = lax.rem(pair + 1, pairs) // self.groups
            l_then = lax.rem(pair + 2, pairs) // self.groups

            @pl.when(mine_next)
            def _():
                self.finish_c(l_next, me)

            @pl.when(mine != lax.rem(pair, self.groups))
            def _():
                self.wait_piece(pair, side)

            @pl.when(mine_next)
            def _():
                solved = mul_nt(self.x[pair, self.rows(side)], self.ph[l_next], self.pl[l_next])
                self.emit(l_next, me, self.c[l_next] - solved)

            self.wait_piece(pair, 1 - side)
            self.update(pair, me)

            @pl.when(mine_then)
            def _():
                self.start_c(l_then, me)

            return carry

        lax.fori_loop(0, pairs, step, 0)

    def write(self, me, pivots):
        for l in range(2):
            for other in range(2):
                @pl.when(lax.rem(me, 2) == other)
                def _(l=l, other=other):
                    pivots[l] = self.x[l * self.groups + me // 2, :, 128 * other : 128 * (other + 1)]

    def wait_sends(self, me):
        q, side = lax.rem(me, 2), self.side(me)
        for l in range(2):
            for order, to in self.targets(me):
                self.piece(l * self.groups + me // 2, side, to, self.xs.at[l, order]).wait_send()
            self.copy_d(l, me).wait_send()
            self.copy_r(l, q, me).wait_send()
            self.copy_b(l, q, me).wait_send()

            @pl.when(q == 1)
            def _(l=l):
                self.copy_t(l, me).wait_send()


SPAN = 4


class Root(Front):
    def place(self, me):
        return me // SPAN, lax.rem(me, SPAN)

    def beside(self, me, step):
        y, q = self.place(me)
        return y * SPAN + lax.rem(q + step, SPAN)

    def z_tile(self, l, q, to, step):
        return pltpu.make_async_remote_copy(
            self.zall.at[l, self.my_leaf, q], self.zall.at[l, self.my_leaf, q],
            self.zs.at[l, step], self.zr.at[l, q],
            device_id={"tile": to}, device_id_type=MESH,
        )

    def z_leaf(self, l, which, there, sends, step):
        return pltpu.make_async_remote_copy(
            self.zall.at[l, which], self.zall.at[l, which], sends.at[l, step], self.gr.at[l, which],
            device_id={"leaf": there}, device_id_type=MESH,
        )

    def partner(self):
        return self.my_leaf + 1 - 2 * lax.rem(self.my_leaf, 2)

    def solve_z(self, l, me):
        y, q = self.place(me)
        group = l * self.groups + y
        column = SPAN * jnp.maximum(group - 1, 0) + jnp.minimum(self.my_leaf, SPAN - 1)
        shape = (128, 128)
        same = lax.broadcasted_iota(jnp.int32, shape, 0) == lax.broadcasted_iota(jnp.int32, shape, 1)
        unit = same.astype(F32) * (self.my_leaf - SPAN == q).astype(F32)
        self.zwork[...] = jnp.where(self.my_leaf < SPAN, self.tile(l, column), unit)
        for before in range(SPAN - 1):
            @pl.when(before < q)
            def _(before=before):
                inner = self.tile(l, SPAN * group + before)
                self.z_tile(l, before, me, 0).wait_recv()
                known = self.zall[l, self.my_leaf, before]
                self.zwork[...] = self.zwork[...] - mul_nn(inner, known)

        self.zall[l, self.my_leaf, q] = mul_nn(self.inverse[l], self.zwork[...])
        for step in range(1, SPAN):
            self.z_tile(l, q, self.beside(me, step), step).start()

    def send_over_x(self, l, me):
        q = lax.rem(me, SPAN)
        for after in range(1, SPAN):
            @pl.when(after > q)
            def _(after=after):
                self.z_tile(l, after, me, 0).wait_recv()

        for step in range(2, self.leaves, 2):
            there = lax.rem(self.my_leaf + step, self.leaves)
            self.z_leaf(l, self.my_leaf, there, self.gs, step).start()

    def send_to_core(self, l):
        for step in range(0, self.leaves, 2):
            which = lax.rem(self.my_leaf + step, self.leaves)
            if step:
                self.z_leaf(l, which, which, self.gs, step).wait_recv()
            self.z_leaf(l, which, self.partner(), self.ks, step).start()

    def take_z(self, l):
        for step in range(0, self.leaves, 2):
            which = lax.rem(self.partner() + step, self.leaves)
            self.z_leaf(l, which, which, self.ks, step).wait_recv()
        for g in range(2 * SPAN):
            at = slice(128 * (g % SPAN), 128 * (g % SPAN + 1))
            for q in range(SPAN):
                row = slice(128 * q, 128 * (q + 1))
                if g < SPAN:
                    self.ph[l, row, at], self.pl[l, row, at] = split(self.zall[l, g, q])
                else:
                    self.gh[l, row, at], self.gl[l, row, at] = split(self.zall[l, g, q])

    def send_group(self, l, me, down):
        y, q = self.place(me)
        group = l * self.groups + y
        to = lax.rem(y + down, self.groups) * SPAN + q
        return pltpu.make_async_remote_copy(
            self.x.at[group], self.x.at[group], self.xs.at[l, down], self.xr.at[group],
            device_id={"tile": to}, device_id_type=MESH,
        )

    def emit(self, l, me, solved):
        self.x[l * self.groups + me // SPAN] = solved
        for down in range(1, self.groups):
            self.send_group(l, me, down).start()

    def arrive(self, group, me):
        @pl.when(me // SPAN != lax.rem(group, self.groups))
        def _():
            pltpu.make_async_remote_copy(
                self.x.at[group], self.x.at[group], self.xs.at[0, 0], self.xr.at[group],
                device_id={"tile": 0}, device_id_type=MESH,
            ).wait_recv()

    def copy_b(self, l, q, to, step):
        return pltpu.make_async_remote_copy(
            self.bin.at[l, q], self.bin.at[l, q], self.bs.at[l, step], self.br.at[l, q],
            device_id={"tile": to}, device_id_type=MESH,
        )

    def start_c(self, l, me):
        q = lax.rem(me, SPAN)
        self.bin[l, q] = self.b[l]
        for step in (2, 1, 3):
            self.copy_b(l, q, self.beside(me, step), step).start()

    def finish_c(self, l, me):
        for step in (1, 3, 2):
            q = lax.rem(me + step, SPAN)
            self.copy_b(l, q, me, 0).wait_recv()
        whole = jnp.concatenate([self.bin[l, other] for other in range(SPAN)], 1)
        self.c[l] = mul_nt(whole, self.gh[l], self.gl[l])

    def update(self, group, me):
        now = self.x[group]
        out = mul_nt(now[:, :256], self.wh[2 * group], self.wl[2 * group])
        out = out + mul_nt(now[:, 256:], self.wh[2 * group + 1], self.wl[2 * group + 1])
        for l in range(self.b.shape[0]):
            part = out[:, 128 * l : 128 * (l + 1)]
            if l < 2:
                part = part * (l * self.groups + me // SPAN > group + 1).astype(F32)
            self.b[l] = self.b[l] - part

    def run(self, me):
        groups = 2 * self.groups
        y = me // SPAN

        @pl.when(y < 2)
        def _():
            self.start_c(0, me)

        @pl.when(y == 0)
        def _():
            self.finish_c(0, me)
            self.emit(0, me, self.c[0])

        def step(group, carry):
            mine_next = jnp.logical_and(group + 1 < groups, y == lax.rem(group + 1, self.groups))
            mine_then = jnp.logical_and(group + 2 < groups, y == lax.rem(group + 2, self.groups))
            l_next = lax.rem(group + 1, groups) // self.groups
            l_then = lax.rem(group + 2, groups) // self.groups

            @pl.when(mine_next)
            def _():
                self.finish_c(l_next, me)

            self.arrive(group, me)

            @pl.when(mine_next)
            def _():
                solved = mul_nt(self.x[group], self.ph[l_next], self.pl[l_next])
                self.emit(l_next, me, self.c[l_next] - solved)

            self.update(group, me)

            @pl.when(group == 0)
            def _():
                self.send_to_core(1)

            @pl.when(group == 1)
            def _():
                self.take_z(1)

            @pl.when(mine_then)
            def _():
                self.start_c(l_then, me)

            return carry

        lax.fori_loop(0, groups, step, 0)

    def write(self, me, pivots):
        y, q = self.place(me)
        for l in range(2):
            for other in range(SPAN):
                @pl.when(other == q)
                def _(l=l, other=other):
                    pivots[l] = self.x[l * self.groups + y, :, 128 * other : 128 * (other + 1)]

    def wait_sends(self, me):
        q = lax.rem(me, SPAN)
        for l in range(2):
            for down in range(1, self.groups):
                self.send_group(l, me, down).wait_send()
            for step in range(1, SPAN):
                self.copy_b(l, q, self.beside(me, step), step).wait_send()
                self.z_tile(l, q, self.beside(me, step), step).wait_send()
            for step in range(0, self.leaves, 2):
                which = lax.rem(self.my_leaf + step, self.leaves)
                if step:
                    self.z_leaf(l, self.my_leaf, which, self.gs, step).wait_send()
                self.z_leaf(l, which, self.partner(), self.ks, step).wait_send()


def kernel(sizes, *refs):
    tiles, leaves, blocks, sources = sizes
    share = sources // leaves
    names_in = ("forcing", "inverse", "dense", "slot", "left", "right", "rank")
    leaf_in = dict(zip(names_in, refs[:7]))
    place = refs[7]
    root_in = dict(zip(names_in, refs[8:15]))
    leaf_pivots, root_pivots, root_updates = refs[15:18]
    scratch = list(refs[18:])
    me = lax.axis_index("tile")
    my_leaf = lax.axis_index("leaf")
    even_steps, odd_steps = [3, 4, 5, 2, 1], [1, 4, 3, 2, tiles - 1]
    for steps in (even_steps, odd_steps):
        steps[:] = list(dict.fromkeys(s for s in steps + list(range(1, tiles)) if 0 < s < tiles))
    order = list(zip(even_steps, odd_steps))

    common = (
        "b", "x", "c", "wh", "wl", "inverse", "dense", "left", "right", "xs", "xr", "load", "ph", "pl",
    )
    for_leaf = (
        "gh", "gl", "bin", "bout", "dother", "inner", "outer", "bmat",
        "ds", "dr", "ts", "tr", "rs", "rr", "bs", "br",
    )
    for_root = (
        "gh", "gl", "bin", "zall", "zwork", "zs", "zr", "gs", "ks", "gr", "bs", "br",
    )

    def front_of(kind, inputs, names, groups, **more):
        mine = {name: scratch.pop(0) for name in names}
        return kind(
            slot=inputs["slot"], rank=inputs["rank"], tiles=tiles, groups=groups, **more, **mine
        )

    leaf = front_of(
        Leaf, leaf_in, common + for_leaf, tiles // 2, steps=order, half=sources // 2
    )
    root = front_of(
        Root, root_in, common + for_root, tiles // SPAN, leaves=leaves, my_leaf=my_leaf
    )
    root_forcing, sum_out, sum_in, sum_send, sum_recv = scratch

    def load(front, inputs, forcing):
        pairs = [(inputs["forcing"], forcing)] + [
            (inputs[n], getattr(front, n)) for n in ("inverse", "left", "right", "dense")
        ]
        return [
            pltpu.make_async_copy(src, dst, front.load.at[n]) for n, (src, dst) in enumerate(pairs)
        ]

    leaf_loads = load(leaf, leaf_in, leaf.b)
    root_loads = load(root, root_in, root_forcing)
    for copy in leaf_loads:
        copy.start()
    for copy in root_loads:
        copy.start()

    barrier = pltpu.get_barrier_semaphore()
    for step in range(1, tiles):
        pl.semaphore_signal(
            barrier, inc=1, device_id={"tile": lax.rem(me + step, tiles)}, device_id_type=MESH
        )
    for step in range(1, leaves):
        pl.semaphore_signal(
            barrier, inc=1, device_id={"leaf": lax.rem(my_leaf + step, leaves)}, device_id_type=MESH
        )
    for copy in leaf_loads:
        copy.wait()
    pl.semaphore_wait(barrier, tiles + leaves - 2)

    leaf.start(me)
    for copy in root_loads:
        copy.wait()

    def beside(pair):
        leaf.prepare(pair)
        root.prepare(pair)

        @pl.when(pair == 1)
        def _():
            leaf.share_inner(1, me)
            leaf.share_outer(1, me)

        @pl.when(pair == SPAN + 1)
        def _():
            leaf.make_g(1, me)
            leaf.make_p(1, me)


        y, q = root.place(me)

        @pl.when(pair == 1 + 2 * q)
        def _():
            root.solve_z(0, me)

        @pl.when(pair == 3 + 2 * q + 2)
        def _():
            root.solve_z(1, me)

        @pl.when(pair == 9)
        def _():
            root.send_over_x(0, me)

        @pl.when(pair == 13)
        def _():
            root.send_over_x(1, me)

        @pl.when(pair == 15)
        def _():
            root.send_to_core(0)

    leaf.run(me, beside)

    leaf.write(me, leaf_pivots)

    for m in range(blocks):
        part = jnp.zeros((sources, 128), F32)
        for u in range(2):
            part = part + leaf.b[2 + u] * (place[0, 0, u] == m).astype(F32)
        for g in range(leaves):
            sum_out[g, m] = part[share * g : share * (g + 1)]

    def sum_copy(step, there):
        return pltpu.make_async_remote_copy(
            sum_out.at[there], sum_in.at[my_leaf], sum_send.at[step], sum_recv.at[my_leaf],
            device_id={"leaf": there}, device_id_type=MESH,
        )

    def sum_wait(here):
        return pltpu.make_async_remote_copy(
            sum_out.at[here], sum_in.at[here], sum_send.at[0], sum_recv.at[here],
            device_id={"leaf": here}, device_id_type=MESH,
        )

    for step in range(1, leaves):
        sum_copy(step, lax.rem(my_leaf + step, leaves)).start()
    for m in range(blocks):
        mine = root_forcing[m, pl.ds(pl.multiple_of(my_leaf * share, share), share)]
        root.b[m] = mine + sum_out[my_leaf, m]
    root.take_z(0)
    for step in range(1, leaves):
        here = lax.rem(my_leaf + step, leaves)
        sum_wait(here).wait_recv()
        for m in range(blocks):
            root.b[m] = root.b[m] + sum_in[here, m]

    root.run(me)
    root.write(me, root_pivots)
    for l in range(2):
        root_updates[l] = root.b[2 + l]

    leaf.wait_sends(me)
    root.wait_sends(me)
    for step in range(1, leaves):
        sum_copy(step, lax.rem(my_leaf + step, leaves)).wait_send()


def common_scratch(tiles, blocks, sources, dense_count, rank, x, c, p):
    pivots = 2 * tiles
    blk = 128
    vmem = pltpu.VMEM
    dma = pltpu.SemaphoreType.DMA
    return [
        vmem((blocks, sources, blk), F32),
        vmem(x, F32),
        vmem(c, F32),
        vmem((tiles, blocks * blk, 2 * blk), BF16),
        vmem((tiles, blocks * blk, 2 * blk), BF16),
        vmem((2, blk, blk), F32),
        vmem((dense_count, blk, blk), F32),
        vmem((blocks, pivots, rank, blk), F32),
        vmem((blocks, pivots, rank, blk), F32),
        dma((2, tiles)),
        dma((pivots,)),
        dma((5,)),
        vmem(p, BF16),
        vmem(p, BF16),
    ]


def leaf_scratch(sources):
    blk = 128
    vmem = pltpu.VMEM
    dma = pltpu.SemaphoreType.DMA
    return [
        vmem((2, 2 * blk, 2 * blk), BF16),
        vmem((2, 2 * blk, 2 * blk), BF16),
        vmem((2, 2, sources // 2, blk), F32),
        vmem((2, sources // 2, blk), F32),
        vmem((2, blk, blk), F32),
        vmem((2, blk, blk), F32),
        vmem((2, 2, blk, 2 * blk), F32),
        vmem((2, blk, blk), F32),
    ] + [dma((2,))] * 8


def root_scratch(sources, leaves):
    blk = 128
    vmem = pltpu.VMEM
    dma = pltpu.SemaphoreType.DMA
    return [
        vmem((2, SPAN * blk, SPAN * blk), BF16),
        vmem((2, SPAN * blk, SPAN * blk), BF16),
        vmem((2, SPAN, sources, blk), F32),
        vmem((2, leaves, SPAN, blk, blk), F32),
        vmem((blk, blk), F32),
        dma((2, SPAN)),
        dma((2, SPAN)),
        dma((2, leaves)),
        dma((2, leaves)),
        dma((2, leaves)),
        dma((2, SPAN)),
        dma((2, SPAN)),
    ]


def hand_over(*refs):
    for source, result in zip(refs[:3], refs[3:]):
        result[...] = source[...]


def body(
    forcing_leaf,
    inverse_leaf,
    dense_leaf,
    slot_leaf,
    left_leaf,
    right_leaf,
    rank_leaf,
    place_leaf,
    forcing_root,
    inverse_root,
    dense_root,
    slot_root,
    left_root,
    right_root,
    rank_root,
):
    tiles = lax.axis_size("tile")
    leaves = lax.axis_size("leaf")
    blocks, sources, blk = forcing_leaf.shape[1], forcing_leaf.shape[3], forcing_leaf.shape[4]
    dense_count, rank = dense_leaf.shape[2], left_leaf.shape[4]
    share = sources // leaves
    args = (
        forcing_leaf[0, :, 0],
        inverse_leaf[0, :, 0],
        dense_leaf[0, 0],
        slot_leaf,
        left_leaf[0, :, 0],
        right_leaf[0, :, 0],
        rank_leaf,
        place_leaf.transpose(0, 2, 1),
        forcing_root[:, 0],
        inverse_root[:, 0],
        dense_root[0],
        slot_root[None],
        left_root[:, 0],
        right_root[:, 0],
        rank_root[None],
    )
    smem = pl.BlockSpec(memory_space=pltpu.SMEM)
    hbm = pl.BlockSpec(memory_space=pl.ANY)
    vmem = pl.BlockSpec(memory_space=pltpu.VMEM)
    one = [hbm, hbm, hbm, smem, hbm, hbm, smem]
    shapes = (
        jax.ShapeDtypeStruct((2, sources, blk), F32),
        jax.ShapeDtypeStruct((2, share, blk), F32),
        jax.ShapeDtypeStruct((2, share, blk), F32),
    )
    solved = pl.pallas_call(
        functools.partial(kernel, (tiles, leaves, blocks, sources)),
        out_shape=shapes,
        in_specs=one + [smem] + one,
        out_specs=(vmem, vmem, vmem),
        scratch_shapes=common_scratch(
            tiles, blocks, sources, dense_count, rank,
            (tiles, sources, 2 * blk), (2, sources // 2, 2 * blk), (2, 2 * blk, 2 * blk),
        )
        + leaf_scratch(sources)
        + common_scratch(
            tiles, blocks, share, dense_count, rank,
            (2 * tiles // SPAN, share, SPAN * blk), (2, share, SPAN * blk), (2, SPAN * blk, SPAN * blk),
        )
        + root_scratch(share, leaves)
        + [
            pltpu.VMEM((blocks, sources, blk), F32),
            pltpu.VMEM((leaves, blocks, share, blk), F32),
            pltpu.VMEM((leaves, blocks, share, blk), F32),
            pltpu.SemaphoreType.DMA((leaves,)),
            pltpu.SemaphoreType.DMA((leaves,)),
        ],
        compiler_params=pltpu.CompilerParams(
            collective_id=0, has_side_effects=True, vmem_limit_bytes=60 * 2**20
        ),
    )(*args)
    leaf_pivots, root_pivots, root_updates = pl.pallas_call(
        hand_over, out_shape=shapes, in_specs=[vmem] * 3, out_specs=(vmem, vmem, vmem)
    )(*solved)
    return leaf_pivots[None, :, None], root_pivots[:, None], root_updates[:, None]


def solution(mesh):
    placed = (
        P("leaf", None, "tile", None, None),
        P("leaf", None, "tile", None, None),
        P("leaf", "tile", None, None, None),
        P("leaf", None, "tile", None),
        P("leaf", None, "tile", None, None, None),
        P("leaf", None, "tile", None, None, None),
        P("leaf", None, "tile", None),
        P("leaf", None, "tile"),
        P(None, "tile", None, None),
        P(None, "tile", None, None),
        P("tile", None, None, None),
        P(None, "tile", None),
        P(None, "tile", None, None, None),
        P(None, "tile", None, None, None),
        P(None, "tile", None),
    )
    return jax.shard_map(
        body,
        mesh=mesh,
        in_specs=placed,
        out_specs=(
            P("leaf", None, "tile", None, None),
            P(None, "tile", "leaf", None),
            P(None, "tile", "leaf", None),
        ),
        check_vma=False,
    )
```

```python
import functools

import jax
import jax.numpy as jnp
from jax import lax
from jax.experimental import pallas as pl
from jax.experimental.pallas import tpu as pltpu
from jax.sharding import PartitionSpec as P

F32 = jnp.float32
BF16 = jnp.bfloat16
MESH = pl.DeviceIdType.MESH


def split(a):
    high = a.astype(BF16)
    return high, (a - high.astype(F32)).astype(BF16)


def dot_nn(a, b):
    return lax.dot_general(a, b, (((1,), (0,)), ((), ())), preferred_element_type=F32)


def dot_nt(a, b):
    return lax.dot_general(a, b, (((1,), (1,)), ((), ())), preferred_element_type=F32)


def mul_nn(a, b):
    ah, al = split(a)
    bh, bl = split(b)
    return dot_nn(jnp.concatenate([ah, al], 1), jnp.concatenate([bh, bh], 0)) + dot_nn(ah, bl)


def mul_nt(x, wh, wl):
    rows = x.shape[0]
    xh = x.astype(BF16)
    xhf = xh.astype(F32)
    both = jnp.concatenate([xhf, x - xhf], 0).astype(BF16)
    first = dot_nt(both, wh)
    return first[:rows] + first[rows:] + dot_nt(xh, wl)


class Front:
    def __init__(self, **refs):
        self.__dict__.update(refs)

    def masked_right(self, l, k):
        right = self.right[l, k]
        row = lax.broadcasted_iota(jnp.int32, right.shape, 0)
        return jnp.where(row < self.rank[0, l, 0, k], right, 0.0)

    def choose(self, l, k, low):
        slot = self.slot[0, l, 0, k]
        dense = self.dense[jnp.maximum(slot, 0)]
        return jnp.where(slot >= 0, dense, low)

    def tile(self, l, k):
        left = self.left[l, k]
        lh = left.astype(BF16).astype(F32)
        rh, rl = split(self.masked_right(l, k))
        zero = jnp.zeros_like(left)
        cols = jnp.concatenate([lh, left - lh, lh, zero], 0).T.astype(BF16)
        rows = jnp.concatenate([rh, rh, rl, zero.astype(BF16)], 0)
        return self.choose(l, k, dot_nn(cols, rows))

    def prepare_column(self, pair, half):
        k = 2 * pair + half
        blocks = self.left.shape[0]
        lt = jnp.concatenate([self.left[l, k] for l in range(blocks)], 0).T
        lh, ll = split(lt)
        rights = [split(self.masked_right(l, k)) for l in range(blocks)]

        def diagonal(part):
            zero = jnp.zeros_like(rights[0][0])
            return jnp.concatenate(
                [
                    jnp.concatenate([rights[l][part] if m == l else zero for m in range(blocks)], 1)
                    for l in range(blocks)
                ],
                0,
            )

        rh, rl = diagonal(0), diagonal(1)
        low = dot_nn(jnp.concatenate([lh, ll], 1), jnp.concatenate([rh, rh], 0)) + dot_nn(lh, rl)
        for l in range(blocks):
            th, tl = split(self.choose(l, k, low[:, 128 * l : 128 * (l + 1)]))
            self.wh[pair, 128 * l : 128 * (l + 1), 128 * half : 128 * (half + 1)] = th
            self.wl[pair, 128 * l : 128 * (l + 1), 128 * half : 128 * (half + 1)] = tl

    def prepare(self, pair):
        self.prepare_column(pair, 0)
        self.prepare_column(pair, 1)


class Leaf(Front):
    def partner(self, me):
        return me + 1 - 2 * lax.rem(me, 2)

    def side(self, me):
        return lax.rem(lax.rem(me, 4) + 1, 4) // 2

    def rows(self, side):
        return pl.ds(pl.multiple_of(side * self.half, self.half), self.half)

    def targets(self, me):
        odd = lax.rem(me, 2)
        for order, (to_even, to_odd) in enumerate(self.steps):
            yield order, lax.rem(me + to_even + (to_odd - to_even) * odd, self.tiles)

    def piece(self, pair, side, to, sem):
        part = self.x.at[pair, self.rows(side)]
        return pltpu.make_async_remote_copy(
            part, part, sem, self.xr.at[2 * pair + side],
            device_id={"tile": to}, device_id_type=MESH,
        )

    def send(self, source, target, sends, recvs, at, me):
        return pltpu.make_async_remote_copy(
            source, target, sends.at[at], recvs.at[at],
            device_id={"tile": self.partner(me)}, device_id_type=MESH,
        )

    def copy_d(self, l, me):
        return self.send(self.inverse.at[l], self.dother.at[l], self.ds, self.dr, l, me)

    def copy_t(self, l, me):
        return self.send(self.inner.at[l], self.inner.at[l], self.ts, self.tr, l, me)

    def copy_r(self, l, q, me):
        return pltpu.make_async_remote_copy(
            self.outer.at[l, q], self.outer.at[l, q], self.rs.at[l], self.rr.at[l],
            device_id={"tile": self.partner(me)}, device_id_type=MESH,
        )

    def copy_b(self, l, q, me):
        return pltpu.make_async_remote_copy(
            self.bout.at[l], self.bin.at[l, q], self.bs.at[l], self.br.at[l],
            device_id={"tile": self.partner(me)}, device_id_type=MESH,
        )

    def share_inner(self, l, me):
        self.copy_d(l, me).start()

        @pl.when(lax.rem(me, 2) == 1)
        def _():
            self.inner[l] = self.tile(l, 2 * (l * self.groups + me // 2))
            self.copy_t(l, me).start()

    def share_outer(self, l, me):
        prev = jnp.maximum(l * self.groups + me // 2 - 1, 0)
        q = lax.rem(me, 2)
        for half in range(2):
            self.outer[l, q, :, 128 * half : 128 * (half + 1)] = self.tile(l, 2 * prev + half)
        self.copy_r(l, q, me).start()

    def diagonals(self, l, me):
        even = lax.rem(me, 2) == 0
        mine, other = self.inverse[l], self.dother[l]
        return jnp.where(even, mine, other), jnp.where(even, other, mine)

    def make_g(self, l, me):
        self.copy_d(l, me).wait_recv()

        @pl.when(lax.rem(me, 2) == 0)
        def _():
            self.copy_t(l, me).wait_recv()

        first, second = self.diagonals(l, me)
        between = mul_nn(second, self.inner[l])
        self.bmat[l] = between
        zero = jnp.zeros((128, 128), BF16)
        low = split(-mul_nn(between, first))
        for ref, top, left, right in zip((self.gh, self.gl), split(first), low, split(second)):
            ref[l, :128, :128] = top
            ref[l, :128, 128:] = zero
            ref[l, 128:, :128] = left
            ref[l, 128:, 128:] = right

    def make_p(self, l, me):
        self.copy_r(l, 1 - lax.rem(me, 2), me).wait_recv()
        first, second = self.diagonals(l, me)
        top = mul_nn(first, self.outer[l, 0])
        bottom = mul_nn(second, self.outer[l, 1]) - mul_nn(self.bmat[l], top)
        self.ph[l, :128], self.pl[l, :128] = split(top)
        self.ph[l, 128:], self.pl[l, 128:] = split(bottom)

    def start_c(self, l, me):
        q, side = lax.rem(me, 2), self.side(me)
        self.bout[l] = self.b[l, self.rows(1 - side)]
        self.copy_b(l, q, me).start()
        self.bin[l, q] = self.b[l, self.rows(side)]

    def finish_c(self, l, me):
        self.copy_b(l, lax.rem(me, 2), me).wait_recv()
        whole = jnp.concatenate([self.bin[l, 0], self.bin[l, 1]], 1)
        self.c[l] = mul_nt(whole, self.gh[l], self.gl[l])

    def emit(self, l, me, solved):
        pair, side = l * self.groups + me // 2, self.side(me)
        self.x[pair, self.rows(side)] = solved
        for order, to in self.targets(me):
            self.piece(pair, side, to, self.xs.at[l, order]).start()

    def wait_piece(self, pair, side):
        self.piece(pair, side, 0, self.xs.at[0, 0]).wait_recv()

    def update(self, pair, me):
        out = mul_nt(self.x[pair], self.wh[pair], self.wl[pair])
        for l in range(self.b.shape[0]):
            part = out[:, 128 * l : 128 * (l + 1)]
            if l < 2:
                part = part * (l * self.groups + me // 2 > pair + 1).astype(F32)
            self.b[l] = self.b[l] - part

    def start(self, me):
        mine = me // 2
        self.share_inner(0, me)

        @pl.when(mine < 2)
        def _():
            self.start_c(0, me)

        self.share_outer(0, me)
        self.make_g(0, me)

        @pl.when(mine == 0)
        def _():
            self.finish_c(0, me)
            self.emit(0, me, self.c[0])

        self.make_p(0, me)

    def run(self, me, extra):
        pairs = 2 * self.groups
        mine, side = me // 2, self.side(me)

        def step(pair, carry):
            extra(pair)
            mine_next = jnp.logical_and(pair + 1 < pairs, mine == lax.rem(pair + 1, self.groups))
            mine_then = jnp.logical_and(pair + 2 < pairs, mine == lax.rem(pair + 2, self.groups))
            l_next = lax.rem(pair + 1, pairs) // self.groups
            l_then = lax.rem(pair + 2, pairs) // self.groups

            @pl.when(mine_next)
            def _():
                self.finish_c(l_next, me)

            @pl.when(mine != lax.rem(pair, self.groups))
            def _():
                self.wait_piece(pair, side)

            @pl.when(mine_next)
            def _():
                solved = mul_nt(self.x[pair, self.rows(side)], self.ph[l_next], self.pl[l_next])
                self.emit(l_next, me, self.c[l_next] - solved)

            self.wait_piece(pair, 1 - side)
            self.update(pair, me)

            @pl.when(mine_then)
            def _():
                self.start_c(l_then, me)

            return carry

        lax.fori_loop(0, pairs, step, 0)

    def write(self, me, pivots):
        for l in range(2):
            for other in range(2):
                @pl.when(lax.rem(me, 2) == other)
                def _(l=l, other=other):
                    pivots[l] = self.x[l * self.groups + me // 2, :, 128 * other : 128 * (other + 1)]

    def wait_sends(self, me):
        q, side = lax.rem(me, 2), self.side(me)
        for l in range(2):
            for order, to in self.targets(me):
                self.piece(l * self.groups + me // 2, side, to, self.xs.at[l, order]).wait_send()
            self.copy_d(l, me).wait_send()
            self.copy_r(l, q, me).wait_send()
            self.copy_b(l, q, me).wait_send()

            @pl.when(q == 1)
            def _(l=l):
                self.copy_t(l, me).wait_send()


SPAN = 4


class Root(Front):
    def place(self, me):
        return me // SPAN, lax.rem(me, SPAN)

    def beside(self, me, step):
        y, q = self.place(me)
        return y * SPAN + lax.rem(q + step, SPAN)

    def z_slot(self, which):
        return 2 * SPAN + self.my_leaf // 2 if which else self.my_leaf

    def z_tile(self, l, which, q, to, step):
        part = self.zall.at[l, self.z_slot(which), q]
        return pltpu.make_async_remote_copy(
            part, part, self.zs.at[2 * l + which, step], self.zr.at[2 * l + which, q],
            device_id={"tile": to}, device_id_type=MESH,
        )

    def z_leaf(self, l, which, owner, there, sends, step):
        slot = 2 * SPAN + owner // 2 if which else owner
        part = self.zall.at[l, slot]
        return pltpu.make_async_remote_copy(
            part, part, sends.at[2 * l + which, step], self.gr.at[l, slot],
            device_id={"leaf": there}, device_id_type=MESH,
        )

    def partner(self):
        return self.my_leaf + 1 - 2 * lax.rem(self.my_leaf, 2)

    def parts(self, owner, do):
        do(0)

        @pl.when(lax.rem(owner, 2) == 0)
        def _():
            do(1)

    def solve_z(self, l, me):
        y, q = self.place(me)
        group = l * self.groups + y

        def one(which):
            block = self.my_leaf // 2 if which else jnp.minimum(self.my_leaf, SPAN - 1)
            column = SPAN * jnp.maximum(group - 1 - which, 0) + block
            start = self.tile(l, column)
            if which == 0:
                shape = (128, 128)
                down = lax.broadcasted_iota(jnp.int32, shape, 0)
                right = lax.broadcasted_iota(jnp.int32, shape, 1)
                unit = (down == right).astype(F32) * (self.my_leaf - SPAN == q).astype(F32)
                start = jnp.where(self.my_leaf < SPAN, start, unit)
            self.zwork[...] = start
            for before in range(SPAN - 1):
                @pl.when(before < q)
                def _(before=before):
                    inner = self.tile(l, SPAN * group + before)
                    self.z_tile(l, which, before, me, 0).wait_recv()
                    known = self.zall[l, self.z_slot(which), before]
                    self.zwork[...] = self.zwork[...] - mul_nn(inner, known)

            self.zall[l, self.z_slot(which), q] = mul_nn(self.inverse[l], self.zwork[...])
            for step in range(1, SPAN):
                self.z_tile(l, which, q, self.beside(me, step), step).start()

        self.parts(self.my_leaf, one)

    def send_over_x(self, l, me):
        q = lax.rem(me, SPAN)

        def one(which):
            for after in range(1, SPAN):
                @pl.when(after > q)
                def _(after=after):
                    self.z_tile(l, which, after, me, 0).wait_recv()

            for step in range(2, self.leaves, 2):
                there = lax.rem(self.my_leaf + step, self.leaves)
                self.z_leaf(l, which, self.my_leaf, there, self.gs, step).start()

        self.parts(self.my_leaf, one)

    def send_to_core(self, l):
        for step in range(0, self.leaves, 2):
            owner = lax.rem(self.my_leaf + step, self.leaves)

            def one(which, step=step, owner=owner):
                if step:
                    self.z_leaf(l, which, owner, owner, self.gs, step).wait_recv()
                self.z_leaf(l, which, owner, self.partner(), self.ks, step).start()

            self.parts(owner, one)

    def take_z(self, l):
        for step in range(0, self.leaves, 2):
            owner = lax.rem(self.partner() + step, self.leaves)

            def one(which, step=step, owner=owner):
                self.z_leaf(l, which, owner, owner, self.ks, step).wait_recv()

            self.parts(owner, one)
        for g in range(3 * SPAN):
            at = slice(128 * (g % SPAN), 128 * (g % SPAN + 1))
            high, low = ((self.ph, self.pl), (self.gh, self.gl), (self.fh, self.fl))[g // SPAN]
            for q in range(SPAN):
                row = slice(128 * q, 128 * (q + 1))
                high[l, row, at], low[l, row, at] = split(self.zall[l, g, q])

    def send_group(self, l, me, down):
        y, q = self.place(me)
        group = l * self.groups + y
        to = lax.rem(y + down, self.groups) * SPAN + q
        return pltpu.make_async_remote_copy(
            self.x.at[group], self.x.at[group], self.xs.at[l, down], self.xr.at[group],
            device_id={"tile": to}, device_id_type=MESH,
        )

    def emit(self, l, me, solved):
        self.x[l * self.groups + me // SPAN] = solved
        for down in range(1, self.groups):
            self.send_group(l, me, down).start()

    def arrive(self, group, me):
        @pl.when(me // SPAN != lax.rem(group, self.groups))
        def _():
            pltpu.make_async_remote_copy(
                self.x.at[group], self.x.at[group], self.xs.at[0, 0], self.xr.at[group],
                device_id={"tile": 0}, device_id_type=MESH,
            ).wait_recv()

    def copy_b(self, l, q, to, step):
        return pltpu.make_async_remote_copy(
            self.bin.at[l, q], self.bin.at[l, q], self.bs.at[l, step], self.br.at[l, q],
            device_id={"tile": to}, device_id_type=MESH,
        )

    def start_c(self, l, me):
        q = lax.rem(me, SPAN)
        self.bin[l, q] = self.b[l]
        for step in (2, 1, 3):
            self.copy_b(l, q, self.beside(me, step), step).start()

    def finish_c(self, l, me):
        for step in (1, 3, 2):
            q = lax.rem(me + step, SPAN)
            self.copy_b(l, q, me, 0).wait_recv()
        whole = jnp.concatenate([self.bin[l, other] for other in range(SPAN)], 1)
        self.c[l] = mul_nt(whole, self.gh[l], self.gl[l])

    def update(self, group, me):
        now = self.x[group]
        out = mul_nt(now[:, :256], self.wh[2 * group], self.wl[2 * group])
        out = out + mul_nt(now[:, 256:], self.wh[2 * group + 1], self.wl[2 * group + 1])
        for l in range(self.b.shape[0]):
            part = out[:, 128 * l : 128 * (l + 1)]
            if l < 2:
                part = part * (l * self.groups + me // SPAN > group + 2).astype(F32)
            self.b[l] = self.b[l] - part

    def run(self, me):
        groups = 2 * self.groups
        y = me // SPAN

        @pl.when(y < 3)
        def _():
            self.start_c(0, me)

        @pl.when(y < 2)
        def _():
            self.finish_c(0, me)

        @pl.when(y == 0)
        def _():
            self.emit(0, me, self.c[0])

        def step(group, carry):
            def mine(ahead):
                here = jnp.logical_and(group + ahead < groups, y == lax.rem(group + ahead, self.groups))
                return here, lax.rem(group + ahead, groups) // self.groups

            mine_next, l_next = mine(1)
            mine_then, l_then = mine(2)
            mine_late, l_late = mine(3)
            self.arrive(group, me)

            @pl.when(mine_next)
            def _():
                solved = mul_nt(self.x[group], self.ph[l_next], self.pl[l_next])
                self.emit(l_next, me, self.c[l_next] - solved)

            self.update(group, me)

            @pl.when(mine_late)
            def _():
                self.start_c(l_late, me)

            @pl.when(group == 0)
            def _():
                self.send_to_core(1)

            @pl.when(group == 2)
            def _():
                self.take_z(1)

            @pl.when(mine_then)
            def _():
                self.finish_c(l_then, me)
                self.c[l_then] = self.c[l_then] - mul_nt(self.x[group], self.fh[l_then], self.fl[l_then])

            return carry

        lax.fori_loop(0, groups, step, 0)

    def write(self, me, pivots):
        y, q = self.place(me)
        for l in range(2):
            for other in range(SPAN):
                @pl.when(other == q)
                def _(l=l, other=other):
                    pivots[l] = self.x[l * self.groups + y, :, 128 * other : 128 * (other + 1)]

    def wait_sends(self, me):
        q = lax.rem(me, SPAN)
        for l in range(2):
            for down in range(1, self.groups):
                self.send_group(l, me, down).wait_send()
            for step in range(1, SPAN):
                self.copy_b(l, q, self.beside(me, step), step).wait_send()

            def own(which, l=l):
                for step in range(1, SPAN):
                    self.z_tile(l, which, q, self.beside(me, step), step).wait_send()
                for step in range(2, self.leaves, 2):
                    there = lax.rem(self.my_leaf + step, self.leaves)
                    self.z_leaf(l, which, self.my_leaf, there, self.gs, step).wait_send()

            self.parts(self.my_leaf, own)
            for step in range(0, self.leaves, 2):
                owner = lax.rem(self.my_leaf + step, self.leaves)

                def passed(which, l=l, step=step, owner=owner):
                    self.z_leaf(l, which, owner, self.partner(), self.ks, step).wait_send()

                self.parts(owner, passed)


def kernel(sizes, *refs):
    tiles, leaves, blocks, sources = sizes
    share = sources // leaves
    names_in = ("forcing", "inverse", "dense", "slot", "left", "right", "rank")
    leaf_in = dict(zip(names_in, refs[:7]))
    place = refs[7]
    root_in = dict(zip(names_in, refs[8:15]))
    leaf_pivots, root_pivots, root_updates = refs[15:18]
    scratch = list(refs[18:])
    me = lax.axis_index("tile")
    my_leaf = lax.axis_index("leaf")
    even_steps, odd_steps = [3, 4, 5, 2, 1], [1, 4, 3, 2, tiles - 1]
    for steps in (even_steps, odd_steps):
        steps[:] = list(dict.fromkeys(s for s in steps + list(range(1, tiles)) if 0 < s < tiles))
    order = list(zip(even_steps, odd_steps))

    common = (
        "b", "x", "c", "wh", "wl", "inverse", "dense", "left", "right", "xs", "xr", "load", "ph", "pl",
    )
    for_leaf = (
        "gh", "gl", "bin", "bout", "dother", "inner", "outer", "bmat",
        "ds", "dr", "ts", "tr", "rs", "rr", "bs", "br",
    )
    for_root = (
        "gh", "gl", "fh", "fl", "bin", "zall", "zwork", "zs", "zr", "gs", "ks", "gr", "bs", "br",
    )

    def front_of(kind, inputs, names, groups, **more):
        mine = {name: scratch.pop(0) for name in names}
        return kind(
            slot=inputs["slot"], rank=inputs["rank"], tiles=tiles, groups=groups, **more, **mine
        )

    leaf = front_of(
        Leaf, leaf_in, common + for_leaf, tiles // 2, steps=order, half=sources // 2
    )
    root = front_of(
        Root, root_in, common + for_root, tiles // SPAN, leaves=leaves, my_leaf=my_leaf
    )
    root_forcing, sum_out, sum_in, sum_send, sum_recv = scratch

    def load(front, inputs, forcing):
        pairs = [(inputs["forcing"], forcing)] + [
            (inputs[n], getattr(front, n)) for n in ("inverse", "left", "right", "dense")
        ]
        return [
            pltpu.make_async_copy(src, dst, front.load.at[n]) for n, (src, dst) in enumerate(pairs)
        ]

    leaf_loads = load(leaf, leaf_in, leaf.b)
    root_loads = load(root, root_in, root_forcing)
    for copy in leaf_loads:
        copy.start()
    for copy in root_loads:
        copy.start()

    barrier = pltpu.get_barrier_semaphore()
    for step in range(1, tiles):
        pl.semaphore_signal(
            barrier, inc=1, device_id={"tile": lax.rem(me + step, tiles)}, device_id_type=MESH
        )
    for step in range(1, leaves):
        pl.semaphore_signal(
            barrier, inc=1, device_id={"leaf": lax.rem(my_leaf + step, leaves)}, device_id_type=MESH
        )
    for copy in leaf_loads:
        copy.wait()
    pl.semaphore_wait(barrier, tiles + leaves - 2)

    leaf.start(me)
    for copy in root_loads:
        copy.wait()

    def beside(pair):
        leaf.prepare(pair)
        root.prepare(pair)

        @pl.when(pair == 1)
        def _():
            leaf.share_inner(1, me)
            leaf.share_outer(1, me)

        @pl.when(pair == SPAN + 1)
        def _():
            leaf.make_g(1, me)
            leaf.make_p(1, me)


        q = lax.rem(me, SPAN)

        @pl.when(pair == 2 + 2 * q)
        def _():
            root.solve_z(0, me)

        @pl.when(pair == 3 + 2 * q)
        def _():
            root.solve_z(1, me)

        @pl.when(pair == 9)
        def _():
            root.send_over_x(0, me)

        @pl.when(pair == 10)
        def _():
            root.send_over_x(1, me)

        @pl.when(pair == 15)
        def _():
            root.send_to_core(0)

    leaf.run(me, beside)

    leaf.write(me, leaf_pivots)

    for m in range(blocks):
        part = jnp.zeros((sources, 128), F32)
        for u in range(2):
            part = part + leaf.b[2 + u] * (place[0, 0, u] == m).astype(F32)
        for g in range(leaves):
            sum_out[g, m] = part[share * g : share * (g + 1)]

    def sum_copy(step, there):
        return pltpu.make_async_remote_copy(
            sum_out.at[there], sum_in.at[my_leaf], sum_send.at[step], sum_recv.at[my_leaf],
            device_id={"leaf": there}, device_id_type=MESH,
        )

    def sum_wait(here):
        return pltpu.make_async_remote_copy(
            sum_out.at[here], sum_in.at[here], sum_send.at[0], sum_recv.at[here],
            device_id={"leaf": here}, device_id_type=MESH,
        )

    for step in range(1, leaves):
        sum_copy(step, lax.rem(my_leaf + step, leaves)).start()
    for m in range(blocks):
        mine = root_forcing[m, pl.ds(pl.multiple_of(my_leaf * share, share), share)]
        root.b[m] = mine + sum_out[my_leaf, m]
    root.take_z(0)
    for step in range(1, leaves):
        here = lax.rem(my_leaf + step, leaves)
        sum_wait(here).wait_recv()
        for m in range(blocks):
            root.b[m] = root.b[m] + sum_in[here, m]

    root.run(me)
    root.write(me, root_pivots)
    for l in range(2):
        root_updates[l] = root.b[2 + l]

    leaf.wait_sends(me)
    root.wait_sends(me)
    for step in range(1, leaves):
        sum_copy(step, lax.rem(my_leaf + step, leaves)).wait_send()


def common_scratch(tiles, blocks, sources, dense_count, rank, x, c, p):
    pivots = 2 * tiles
    blk = 128
    vmem = pltpu.VMEM
    dma = pltpu.SemaphoreType.DMA
    return [
        vmem((blocks, sources, blk), F32),
        vmem(x, F32),
        vmem(c, F32),
        vmem((tiles, blocks * blk, 2 * blk), BF16),
        vmem((tiles, blocks * blk, 2 * blk), BF16),
        vmem((2, blk, blk), F32),
        vmem((dense_count, blk, blk), F32),
        vmem((blocks, pivots, rank, blk), F32),
        vmem((blocks, pivots, rank, blk), F32),
        dma((2, tiles)),
        dma((pivots,)),
        dma((5,)),
        vmem(p, BF16),
        vmem(p, BF16),
    ]


def leaf_scratch(sources):
    blk = 128
    vmem = pltpu.VMEM
    dma = pltpu.SemaphoreType.DMA
    return [
        vmem((2, 2 * blk, 2 * blk), BF16),
        vmem((2, 2 * blk, 2 * blk), BF16),
        vmem((2, 2, sources // 2, blk), F32),
        vmem((2, sources // 2, blk), F32),
        vmem((2, blk, blk), F32),
        vmem((2, blk, blk), F32),
        vmem((2, 2, blk, 2 * blk), F32),
        vmem((2, blk, blk), F32),
    ] + [dma((2,))] * 8


def root_scratch(sources, leaves):
    blk = 128
    vmem = pltpu.VMEM
    dma = pltpu.SemaphoreType.DMA
    return [vmem((2, SPAN * blk, SPAN * blk), BF16)] * 4 + [
        vmem((2, SPAN, sources, blk), F32),
        vmem((2, 3 * SPAN, SPAN, blk, blk), F32),
        vmem((blk, blk), F32),
        dma((4, SPAN)),
        dma((4, SPAN)),
        dma((4, leaves)),
        dma((4, leaves)),
        dma((2, 3 * SPAN)),
        dma((2, SPAN)),
        dma((2, SPAN)),
    ]


def hand_over(*refs):
    for source, result in zip(refs[:3], refs[3:]):
        result[...] = source[...]


def body(
    forcing_leaf,
    inverse_leaf,
    dense_leaf,
    slot_leaf,
    left_leaf,
    right_leaf,
    rank_leaf,
    place_leaf,
    forcing_root,
    inverse_root,
    dense_root,
    slot_root,
    left_root,
    right_root,
    rank_root,
):
    tiles = lax.axis_size("tile")
    leaves = lax.axis_size("leaf")
    blocks, sources, blk = forcing_leaf.shape[1], forcing_leaf.shape[3], forcing_leaf.shape[4]
    dense_count, rank = dense_leaf.shape[2], left_leaf.shape[4]
    share = sources // leaves
    args = (
        forcing_leaf[0, :, 0],
        inverse_leaf[0, :, 0],
        dense_leaf[0, 0],
        slot_leaf,
        left_leaf[0, :, 0],
        right_leaf[0, :, 0],
        rank_leaf,
        place_leaf.transpose(0, 2, 1),
        forcing_root[:, 0],
        inverse_root[:, 0],
        dense_root[0],
        slot_root[None],
        left_root[:, 0],
        right_root[:, 0],
        rank_root[None],
    )
    smem = pl.BlockSpec(memory_space=pltpu.SMEM)
    hbm = pl.BlockSpec(memory_space=pl.ANY)
    vmem = pl.BlockSpec(memory_space=pltpu.VMEM)
    one = [hbm, hbm, hbm, smem, hbm, hbm, smem]
    shapes = (
        jax.ShapeDtypeStruct((2, sources, blk), F32),
        jax.ShapeDtypeStruct((2, share, blk), F32),
        jax.ShapeDtypeStruct((2, share, blk), F32),
    )
    solved = pl.pallas_call(
        functools.partial(kernel, (tiles, leaves, blocks, sources)),
        out_shape=shapes,
        in_specs=one + [smem] + one,
        out_specs=(vmem, vmem, vmem),
        scratch_shapes=common_scratch(
            tiles, blocks, sources, dense_count, rank,
            (tiles, sources, 2 * blk), (2, sources // 2, 2 * blk), (2, 2 * blk, 2 * blk),
        )
        + leaf_scratch(sources)
        + common_scratch(
            tiles, blocks, share, dense_count, rank,
            (2 * tiles // SPAN, share, SPAN * blk), (2, share, SPAN * blk), (2, SPAN * blk, SPAN * blk),
        )
        + root_scratch(share, leaves)
        + [
            pltpu.VMEM((blocks, sources, blk), F32),
            pltpu.VMEM((leaves, blocks, share, blk), F32),
            pltpu.VMEM((leaves, blocks, share, blk), F32),
            pltpu.SemaphoreType.DMA((leaves,)),
            pltpu.SemaphoreType.DMA((leaves,)),
        ],
        compiler_params=pltpu.CompilerParams(
            collective_id=0, has_side_effects=True, vmem_limit_bytes=60 * 2**20
        ),
    )(*args)
    leaf_pivots, root_pivots, root_updates = pl.pallas_call(
        hand_over, out_shape=shapes, in_specs=[vmem] * 3, out_specs=(vmem, vmem, vmem)
    )(*solved)
    return leaf_pivots[None, :, None], root_pivots[:, None], root_updates[:, None]


def solution(mesh):
    placed = (
        P("leaf", None, "tile", None, None),
        P("leaf", None, "tile", None, None),
        P("leaf", "tile", None, None, None),
        P("leaf", None, "tile", None),
        P("leaf", None, "tile", None, None, None),
        P("leaf", None, "tile", None, None, None),
        P("leaf", None, "tile", None),
        P("leaf", None, "tile"),
        P(None, "tile", None, None),
        P(None, "tile", None, None),
        P("tile", None, None, None),
        P(None, "tile", None),
        P(None, "tile", None, None, None),
        P(None, "tile", None, None, None),
        P(None, "tile", None),
    )
    return jax.shard_map(
        body,
        mesh=mesh,
        in_specs=placed,
        out_specs=(
            P("leaf", None, "tile", None, None),
            P(None, "tile", "leaf", None),
            P(None, "tile", "leaf", None),
        ),
        check_vma=False,
    )
```
